32 devices in a mesh: rows: 8 (over z, x), col: 4 (over y, core).
Axes of the slice: x: 2, y: 2, z: 4, core: 2. Of those that a mesh axis runs over, the one named last changes fastest.
Arguments:
- factor_t: bfloat16 [112, 128, 128], P('rows', 'col'), may hold values from -0.25 to 1.25
- intersection_diag: bfloat16 [112, 128, 128], P('rows'), may hold values from -0.25 to 1.25
- intersection_near: bfloat16 [112, 3, 128, 128], P('rows'), may hold values from -0.3125 to 0.3125
- intersection_cross: bfloat16 [112, 4, 128, 128], P('rows'), may hold values from -0.3125 to 0.3125
- near_cols: int32 [112, 3], P('rows'), may hold values from 0 to 111, as said below
- cross_cols: int32 [112, 4], P('rows'), may hold values from 0 to 111, as said below
Outputs:
- refined_diag: bfloat16 [112, 128, 128], P('rows', 'col')
- refined_near: bfloat16 [112, 3, 128, 128], P('rows', None, 'col')
- refined_cross: bfloat16 [112, 4, 128, 128], P('rows', None, 'col')
The draws below stay inside these ranges and needn't reach their ends.
Inputs may be any that keep to these rules, and one draw needn't show every extreme that they name: near_cols[i, k] differs from i by 1 to 14. cross_cols[i, k] lies in the other half of the block rows; the block rows i * 14 to i * 14 + 13 name at most 14 columns in any one group of 14 block rows, and some group is named that often.
All inputs are finite; a program needn't handle non-finite values.
Results may differ from the reference program's by a relative error of at most 0.0056.
Values may be sent and summed in bfloat16 or wider, within the bound.
A program may use at most 64 MiB of HBM per device.

```python
import jax
import jax.numpy as jnp
from jax import lax

B = 128
NEAR = 3
CROSS = 4
ROW_BLOCKS_EACH = 14
NB = 112
HALFDEV = 4
CAP = 14


def draw_factor_t(key, part):
    scale_value = 0.3 / B ** 0.5
    jitter = jax.random.normal(key, (NB, B, B), jnp.float32) * scale_value
    jitter = jnp.clip(jitter, -0.2, 0.2)
    return (jnp.eye(B, dtype=jnp.float32)[None] + jitter).astype(jnp.bfloat16)


def draw_intersection_diag(key, part):
    scale_value = 0.3 / B ** 0.5
    jitter = jax.random.normal(key, (NB, B, B), jnp.float32) * scale_value
    symmetric = jnp.clip((jitter + jnp.swapaxes(jitter, 1, 2)) * 0.7071, -0.2, 0.2)
    return (jnp.eye(B, dtype=jnp.float32)[None] + symmetric).astype(jnp.bfloat16)


def draw_near_cols(key, part):
    key_offset, key_sign = jax.random.split(jax.random.fold_in(key, 11))
    row_ids = jnp.arange(NB, dtype=jnp.int32)[:, None]
    offsets = jax.random.randint(key_offset, (NB, NEAR), 1, ROW_BLOCKS_EACH + 1)
    random_sign = jax.random.randint(key_sign, (NB, NEAR), 0, 2) * 2 - 1
    fixed_sign = jnp.where(jnp.arange(NEAR)[None, :] == 0, 1, -1)
    direction = jnp.where(jnp.arange(NEAR)[None, :] < 2, fixed_sign, random_sign)
    candidate = row_ids + direction * offsets
    outside = (candidate < 0) | (candidate >= NB)
    return jnp.where(outside, row_ids - direction * offsets, candidate).astype(jnp.int32)


def draw_cross_cols(key, part):
    key_perm, key_row = jax.random.split(jax.random.fold_in(key, 23))
    devices = NB // ROW_BLOCKS_EACH
    slots = ROW_BLOCKS_EACH * CROSS
    device_keys = jax.random.split(key_perm, devices)
    chosen = jax.vmap(lambda subkey: jax.random.permutation(subkey, HALFDEV * CAP)[:slots])(device_keys) // CAP
    device_ids = jnp.arange(devices, dtype=jnp.int32)[:, None]
    target = chosen + jnp.where(device_ids < HALFDEV, HALFDEV, 0)
    inside_range = jax.random.randint(key_row, (devices, slots), 0, ROW_BLOCKS_EACH)
    return (target * ROW_BLOCKS_EACH + inside_range).reshape(NB, CROSS).astype(jnp.int32)


def levels(stream_key, dims, cuts, least, largest):
    def one(position, parts):
        draws = jax.random.uniform(jax.random.fold_in(jax.random.fold_in(stream_key, 6), position), (parts,), jnp.float32, least / len(cuts), largest / len(cuts))
        return jnp.repeat(jnp.exp(draws), dims[position] // parts).reshape((-1,) + (1,) * (len(dims) - position - 1))

    level = one(*cuts[0])
    for cut in cuts[1:]:
        level = level * one(*cut)
    return level


def bell_draw(own_key, extent, spread, bound, cuts=(), kind=jnp.bfloat16):
    values = spread * jax.random.normal(own_key, extent, jnp.float32)
    if cuts:
        values = values * levels(own_key, extent, cuts, -0.22, 0.18)
    return jnp.clip(values, -bound, bound).astype(kind)


def setup_inputs(seed: int = 0) -> dict:
    splits = jax.random.split(jax.random.key(seed), 7)
    return {
        "factor_t": draw_factor_t(jax.random.fold_in(splits[6], 71), 0),
        "intersection_diag": draw_intersection_diag(jax.random.fold_in(splits[6], 71), 0),
        "intersection_near": bell_draw(splits[2], (NB, NEAR, B, B), (3 * B) ** -0.5, 0.3125, ((0, 8),)),
        "intersection_cross": bell_draw(splits[3], (NB, CROSS, B, B), (3 * B) ** -0.5, 0.3125, ((0, 8),)),
        "near_cols": draw_near_cols(jax.random.fold_in(splits[6], 71), 0),
        "cross_cols": draw_cross_cols(jax.random.fold_in(splits[6], 71), 0),
    }


def refine_row(local_full_rows, others, blocks, eye_part, diagonal_part):
    product = jnp.einsum("kcb,kab->kca", others, blocks.astype(jnp.float32))
    product = lax.optimization_barrier(product.astype(jnp.bfloat16)).astype(jnp.float32)
    quadratic = jnp.einsum("kca,da->kcd", product, local_full_rows)
    residual_error = lax.optimization_barrier((eye_part - quadratic).astype(jnp.bfloat16)).astype(jnp.float32)
    correction_step = jnp.einsum("kca,ad->kcd", residual_error, local_full_rows)
    return (diagonal_part + 0.5 * correction_step).astype(jnp.bfloat16)


def reference(factor_t, intersection_diag, intersection_near, intersection_cross, near_cols, cross_cols):
    whole = factor_t.astype(jnp.float32)
    identity = jnp.eye(B, dtype=jnp.float32)

    def one_row(items):
        own_block, diagonal_block_matrix, near_blocks, cross_blocks, near_index, cross_index = items
        local_full_rows = own_block.astype(jnp.float32)
        diag_out = refine_row(local_full_rows, local_full_rows[None], diagonal_block_matrix[None], identity, local_full_rows[None])[0]
        near_out = refine_row(local_full_rows, whole[near_index], near_blocks, jnp.float32(0.0), jnp.float32(0.0))
        cross_out = refine_row(local_full_rows, whole[cross_index], cross_blocks, jnp.float32(0.0), jnp.float32(0.0))
        return diag_out, near_out, cross_out

    refined_diag, refined_near, refined_cross = lax.map(one_row, (factor_t, intersection_diag, intersection_near, intersection_cross, near_cols, cross_cols))
    return refined_diag, refined_near, refined_cross
```

```python
import functools

import jax
import jax.numpy as jnp
from jax import lax
from jax.experimental import pallas as pl
from jax.experimental.pallas import tpu as pltpu
from jax.sharding import PartitionSpec as P

F32 = jnp.float32
BF16 = jnp.bfloat16
PARTS = 8
ROW_CUT = (0, 4, 8, 14)
VMEM_LIMIT = 16 * 1024 * 1024
VMEM_ALL = 67043328
SLACK = 96 * 1024
NT = (((1,), (1,)), ((), ()))
TN = (((0,), (0,)), ((), ()))


def dot(a, b, dims=(((1,), (0,)), ((), ()))):
    return lax.dot_general(a, b, dims, preferred_element_type=F32)


def split(rows, parts):
    size = rows // parts
    return [pl.ds(p * size, size) for p in range(parts)]


def refine_kernel(
    n, c, parts,
    factor, s_diag, s_near, s_cross, near_cols, cross_cols,
    w_diag, w_near, w_cross,
    everyone, nearby, g, full, v_diag, v_near, v_cross, near_at, cross_at,
    load_sem, own_sem, edge_sem, col_send, col_recv, near_send, near_recv,
    cross_send, outer_send, mate_send, chain_recv, mate_recv, ready,
):
    per, width, order = factor.shape
    near, cross = v_near.shape[1], v_cross.shape[1]
    half = n // 2
    planes = half // 2
    cut = [per * p // parts for p in range(parts + 1)]
    r = lax.axis_index("rows")
    q = lax.axis_index("col")
    upper = r // half
    is_upper = upper == 1
    m = r - upper * half
    s = m % 2
    d = jnp.where(is_upper, m // 2, planes - 1 - m // 2)
    inmost = d == 0
    beyond = d > 0
    lower_inmost = jnp.logical_and(upper == 0, inmost)
    upper_inmost = jnp.logical_and(is_upper, inmost)
    has_outer = d + 1 < planes
    mate = r + 1 - 2 * s
    target = jnp.where(is_upper, half - 2 + s, half + s)
    outer = jnp.where(is_upper, r + 2, r - 2)
    col_mate = q + 1 - 2 * (q % 2)
    col_cousins = [(q + 2 * k) % c for k in range(1, c // 2)]
    cousins = len(col_cousins)
    origin = jnp.logical_and(r == 0, q == 0)
    CORE, MATE, NEXT, CROSS, COUSIN = 0, 1, 2, 3, 4

    def other_row(e, side):
        return jnp.where(is_upper, half - 2 - 2 * e, half + 2 * e) + side

    loads = [
        pltpu.make_async_copy(s_diag, v_diag, load_sem.at[0]),
        pltpu.make_async_copy(s_near, v_near, load_sem.at[1]),
        pltpu.make_async_copy(s_cross, v_cross, load_sem.at[2]),
        pltpu.make_async_copy(near_cols, near_at, load_sem.at[3]),
        pltpu.make_async_copy(cross_cols, cross_at, load_sem.at[4]),
    ]

    def beside(step):
        return nearby.at[pl.ds((1 + step) * per, per)]

    own_near = pltpu.make_async_copy(factor, beside(0), own_sem.at[0])

    def rows_of(column):
        return pl.ds(pl.multiple_of(column * width, width), width)

    own_full = pltpu.make_async_copy(factor, full.at[:, rows_of(q), :], own_sem.at[1])

    barrier = pltpu.get_barrier_semaphore()

    def signal(sem, **where):
        pl.semaphore_signal(sem, inc=1, device_id=where, device_id_type=pl.DeviceIdType.MESH)

    greets = [
        (jnp.logical_or(q < col_mate, jnp.logical_and(r == 0, col_mate == 0)), {"col": col_mate}),
        (s == 0, {"rows": mate}),
        (jnp.logical_and(upper == 0, m + 2 < half), {"rows": r + 2}),
        (jnp.logical_and(upper == 0, beyond), {"rows": half + s}),
    ] + [(lower_inmost, {"rows": half + 2 * e + s}) for e in range(planes)]
    greets += [(q < column, {"col": column}) for column in col_cousins]
    late_greets = [(jnp.logical_and(is_upper, m + 2 < half), {"rows": r + 2})]
    heard = [jnp.logical_or(q > col_mate, origin), s == 1, m >= 2, is_upper] + [q > column for column in col_cousins]
    heard += [upper_inmost] * (planes - 1)
    answers = [
        (q > col_mate, CORE, {"col": col_mate}),
        (s == 1, MATE, {"rows": mate}),
        (m >= 2, NEXT, {"rows": r - 2}),
    ] + [(upper_inmost, CROSS, {"rows": half - 2 - 2 * e + s}) for e in range(planes)]
    answers += [(q > column, COUSIN + cousins - 1 - k, {"col": column}) for k, column in enumerate(col_cousins)]

    for condition, where in greets:
        pl.when(condition)(functools.partial(signal, barrier, **where))

    own_full.start()
    own_near.start()
    for load in loads:
        load.start()
    with jax.named_scope("bar"):
        pl.semaphore_wait(barrier, sum(x.astype(jnp.int32) for x in heard))
    for condition, where in late_greets:
        pl.when(condition)(functools.partial(signal, barrier, **where))
    for condition, k, where in answers:
        pl.when(condition)(functools.partial(signal, ready.at[k], **where))

    def send(src, dst, send_sem, recv_sem, **where):
        return pltpu.make_async_remote_copy(
            src_ref=src, dst_ref=dst, send_sem=send_sem, recv_sem=recv_sem,
            device_id=where, device_id_type=pl.DeviceIdType.MESH,
        )

    halves = split(per, col_recv.shape[1])

    def column_piece(column, h):
        return full.at[halves[h], rows_of(column), :]

    def slot(row, p):
        return everyone.at[pl.ds(row * per + cut[p], cut[p + 1] - cut[p])]

    crossing = [
        send(
            factor.at[pl.ds(cut[p], cut[p + 1] - cut[p])], slot(r, p),
            cross_send.at[0], chain_recv.at[d, p], rows=target,
        )
        for p in range(parts)
    ]
    toward = 1 - 2 * s
    to_mate = [send(factor, beside(-toward), near_send.at[0], near_recv.at[0], rows=mate)]
    to_core = [
        send(factor.at[halves[h]], column_piece(q, h), col_send.at[0], col_recv.at[q, h], col=col_mate)
        for h in range(len(halves))
    ]
    to_cousins = [
        [
            send(factor.at[halves[h]], column_piece(q, h), col_send.at[0], col_recv.at[q, h], col=column)
            for h in range(len(halves))
        ]
        for k, column in enumerate(col_cousins)
    ]
    firsts = [(is_upper, None, crossing), (s == 1, MATE, to_mate)]
    firsts += [(q > column, COUSIN + k, to_cousins[k]) for k, column in enumerate(col_cousins)]
    firsts += [(q > col_mate, CORE, to_core)]

    def start_all(copies):
        for copy in copies:
            copy.start()

    with jax.named_scope("own"):
        for condition, _, copies in firsts:
            pl.when(condition)(functools.partial(start_all, copies))

        def after_answer(k, copies):
            pl.semaphore_wait(ready.at[k], 1)
            start_all(copies)

        for condition, k, copies in firsts[:0:-1]:
            pl.when(jnp.logical_not(condition))(functools.partial(after_answer, k, copies))
        pl.when(upper == 0)(functools.partial(after_answer, CROSS, crossing))
        pl.when(m + 2 < half)(lambda: pl.semaphore_wait(ready.at[NEXT], 1))

    sent = [(None, copy) for copy in to_mate]

    def landed(ref, sem):
        send(ref, ref, near_send.at[0], sem, rows=mate).wait_recv()

    def spread(e, p):
        ref = slot(other_row(e, s), p)
        return (
            send(ref, ref, outer_send.at[0], chain_recv.at[e, p], rows=outer),
            send(ref, ref, mate_send.at[0], mate_recv.at[e], rows=mate),
        )

    def forward(e, p):
        landed(slot(other_row(e, s), p), chain_recv.at[e, p])
        on, across = spread(e, p)
        pl.when(has_outer)(on.start)
        across.start()

    def pass_near():
        there = beside(toward)
        landed(there, near_recv.at[0])
        condition = jnp.where(s == 1, m >= 2, m + 2 < half)
        copy = send(there, beside(-toward), near_send.at[1], near_recv.at[1], rows=r + 2 * toward)
        pl.when(condition)(copy.start)
        sent.append((condition, copy))

    def arrive_column(column, h):
        landed(column_piece(column, h), col_recv.at[column, h])

    eye = (
        lax.broadcasted_iota(jnp.int32, (width, order), 0) + q * width
        == lax.broadcasted_iota(jnp.int32, (width, order), 1)
    ).astype(F32)

    def prepare(i, carry):
        z_t = full[i]
        own = full[i, rows_of(q), :]
        square = (-0.5 * dot(z_t, z_t, TN)).astype(BF16)
        blocks = [v_near[i, k] for k in range(near)] + [v_cross[i, k] for k in range(cross)]
        for k in range(near + cross):
            g[i, k] = dot(blocks[k], square, TN).astype(BF16)
        product = dot(own, v_diag[i], NT).astype(BF16)
        residual = (eye - dot(product, z_t, NT)).astype(BF16)
        w_diag[i] = (own.astype(F32) + 0.5 * dot(residual, z_t)).astype(BF16)
        return carry

    def rows_from(e):
        return everyone.at[pl.ds(other_row(e, 1 - s) * per, per)]

    chunks = [(e, p) for e in range(planes) for p in range(parts)]

    def forwards(first, last):
        for e, p in chunks[first:last]:
            with jax.named_scope(f"x{e}{p}"):
                forward(e, p)

    def pass_columns():
        for h in range(len(halves)):
            for k, column in enumerate(col_cousins):
                arrive_column(column, h)
                ref = column_piece(column, h)
                send(ref, ref, col_send.at[0], col_recv.at[column, h], col=col_mate).start()

    first_core = q % 2 == 0
    heads = [
        (jnp.logical_and(first_core, upper == 0), 1),
        (jnp.logical_and(first_core, is_upper), 0),
        (jnp.logical_not(first_core), parts - 1),
    ]

    def take(where, third):
        for condition, head in heads:
            pieces = (chunks[:head], chunks[parts:], chunks[head:parts])

            def some():
                for e, p in pieces[third]:
                    with jax.named_scope(f"x{e}{p}"):
                        forward(e, p)
            if pieces[third]:
                pl.when(jnp.logical_and(where, condition))(some)

    beyond_first = jnp.logical_and(beyond, first_core)
    beyond_second = jnp.logical_and(beyond, jnp.logical_not(first_core))

    def spread_rows(step, first, last):
        with jax.named_scope(f"prep{step}"):
            lax.fori_loop(first, last, prepare, 0, unroll=True)

    take(inmost, 0)
    with jax.named_scope("colf"):
        pass_columns()
    take(inmost, 1)
    take(beyond_second, 0)
    take(inmost, 2)
    with jax.named_scope("loads"):
        own_full.wait()
        for load in loads:
            load.wait()
    with jax.named_scope("cols"):
        for h in range(len(halves)):
            arrive_column(col_mate, h)
            for k in range(1, c // 2):
                arrive_column((col_mate + 2 * k) % c, h)

    row_cut = [per * k // 14 for k in ROW_CUT]
    spread_rows(0, row_cut[0], row_cut[1])
    take(beyond_first, 0)
    take(beyond_second, 1)
    with jax.named_scope("near"):
        pass_near()
    spread_rows(1, row_cut[1], row_cut[2])
    take(beyond_first, 1)
    take(beyond, 2)
    spread_rows(2, row_cut[2], row_cut[3])

    with jax.named_scope("nwait"):
        own_near.wait()
        within = jnp.logical_and(m - toward >= 0, m - toward < half)
        edge = jnp.logical_and(jnp.logical_not(within), jnp.logical_and(r - toward >= 0, r - toward < n))
        pl.when(within)(functools.partial(landed, beside(-toward), near_recv.at[1]))

        @pl.when(edge)
        def _():
            landed(rows_from(0), mate_recv.at[0])
            copy = pltpu.make_async_copy(everyone.at[pl.ds((r - toward) * per, per)], beside(-toward), edge_sem.at[0])
            copy.start()
            copy.wait()

    base = (r - 1) * per

    def finish_near(i, carry):
        for k in range(near):
            place = jnp.clip(near_at[k, i] - base, 0, 3 * per - 1)
            w_near[i, k] = dot(nearby[place], g[i, k]).astype(BF16)
        return carry

    def finish_cross(i, carry):
        for k in range(cross):
            w_cross[i, k] = dot(everyone[cross_at[k, i]], g[i, near + k]).astype(BF16)
        return carry

    with jax.named_scope("ndots"):
        lax.fori_loop(0, per, finish_near, 0, unroll=True)
    with jax.named_scope("fin"):
        pl.when(jnp.logical_not(edge))(functools.partial(landed, rows_from(0), mate_recv.at[0]))
        for e in range(1, planes):
            landed(rows_from(e), mate_recv.at[e])
    with jax.named_scope("cdots"):
        lax.fori_loop(0, per, finish_cross, 0, unroll=True)
    with jax.named_scope("sends"):
        def gone(ref, sem):
            send(ref, ref, sem, near_recv.at[0], rows=mate).wait_send()

        gone(everyone.at[pl.ds(0, planes * per)], mate_send.at[0])
        pl.when(has_outer)(functools.partial(gone, everyone.at[pl.ds(0, planes * per)], outer_send.at[0]))
        gone(everyone.at[pl.ds(0, per)], cross_send.at[0])
        gone(everyone.at[pl.ds(0, per * (2 * cousins + 1))], col_send.at[0])
        for condition, copy in sent:
            if condition is None:
                copy.wait_send()
            else:
                pl.when(condition)(copy.wait_send)


def store_kernel(w_diag, w_near, w_cross, o_diag, o_near, o_cross, sem):
    copies = [
        pltpu.make_async_copy(w_diag, o_diag, sem.at[0]),
        pltpu.make_async_copy(w_near, o_near, sem.at[1]),
        pltpu.make_async_copy(w_cross, o_cross, sem.at[2]),
    ]
    for copy in copies:
        copy.start()
    for copy in copies:
        copy.wait()


def body(n, c, factor_t, intersection_diag, intersection_near, intersection_cross, near_cols, cross_cols):
    per, width, order = factor_t.shape
    near, cross = near_cols.shape[1], cross_cols.shape[1]
    planes = n // 4
    parts = max(1, min(PARTS // planes, per))
    col_parts = 2 if per % 2 == 0 else 1
    smem = pltpu.SMEM
    vmem = pl.BlockSpec(memory_space=pltpu.VMEM)
    hbm = pl.BlockSpec(memory_space=pl.ANY)
    dma = pltpu.SemaphoreType.DMA
    shapes = ((per, width, order), (per, near, width, order), (per, cross, width, order))
    kept = 2 * order * width * per * (1 + near + cross)
    results = pl.pallas_call(
        functools.partial(refine_kernel, n, c, parts),
        out_shape=tuple(pltpu.VMEM(shape, BF16) for shape in shapes),
        in_specs=[pl.BlockSpec(memory_space=pltpu.HBM)] * 6,
        out_specs=(vmem,) * 3,
        scratch_shapes=[
            pltpu.VMEM((n * per, width, order), BF16),
            pltpu.VMEM((3 * per, width, order), BF16),
            pltpu.VMEM((per, near + cross, order, order), BF16),
            pltpu.VMEM((per, order, order), BF16),
            pltpu.VMEM(intersection_diag.shape, BF16),
            pltpu.VMEM(intersection_near.shape, BF16),
            pltpu.VMEM(intersection_cross.shape, BF16),
            smem((near, per), jnp.int32),
            smem((cross, per), jnp.int32),
            dma((5,)),
            dma((2,)),
            dma((1,)),
            dma((1,)),
            dma((c, col_parts)),
            dma((2,)),
            dma((2,)),
            dma((1,)),
            dma((1,)),
            dma((1,)),
            dma((planes, parts)),
            dma((planes,)),
            pltpu.SemaphoreType.REGULAR((3 + c // 2,)),
        ],
        compiler_params=pltpu.CompilerParams(
            collective_id=0, has_side_effects=True, vmem_limit_bytes=VMEM_ALL - kept - SLACK,
        ),
    )(factor_t, intersection_diag, intersection_near, intersection_cross, near_cols.T, cross_cols.T)
    return pl.pallas_call(
        store_kernel,
        out_shape=tuple(jax.ShapeDtypeStruct(shape, BF16) for shape in shapes),
        in_specs=[vmem] * 3,
        out_specs=(hbm,) * 3,
        scratch_shapes=[dma((3,))],
        compiler_params=pltpu.CompilerParams(vmem_limit_bytes=VMEM_LIMIT),
    )(*results)


def solution(mesh):
    placed = (
        P("rows", "col", None),
        P("rows", None, None),
        P("rows", None, None, None),
        P("rows", None, None, None),
        P("rows", None),
        P("rows", None),
    )
    return jax.shard_map(
        functools.partial(body, mesh.shape["rows"], mesh.shape["col"]),
        mesh=mesh,
        in_specs=placed,
        out_specs=(
            P("rows", "col", None),
            P("rows", None, "col", None),
            P("rows", None, "col", None),
        ),
        check_vma=False,
    )
```

```python
import functools

import jax
import jax.numpy as jnp
from jax import lax
from jax.experimental import pallas as pl
from jax.experimental.pallas import tpu as pltpu
from jax.sharding import PartitionSpec as P

F32 = jnp.float32
BF16 = jnp.bfloat16
PARTS = 14
ROW_CUT = (0, 5, 10, 14)
VMEM_LIMIT = 16 * 1024 * 1024
VMEM_ALL = 67043328
SLACK = 96 * 1024
NT = (((1,), (1,)), ((), ()))
TN = (((0,), (0,)), ((), ()))


def dot(a, b, dims=(((1,), (0,)), ((), ()))):
    return lax.dot_general(a, b, dims, preferred_element_type=F32)


def split(rows, parts):
    size = rows // parts
    return [pl.ds(p * size, size) for p in range(parts)]


def refine_kernel(
    n, c, parts,
    factor, s_diag, s_near, s_cross, near_cols, cross_cols,
    w_diag, w_near, w_cross,
    everyone, nearby, g, full, v_diag, v_near, v_cross, near_at, cross_at,
    load_sem, own_sem, edge_sem, col_send, col_recv, near_send, near_recv,
    cross_send, outer_send, mate_send, slant_send, chain_recv, mate_recv, ready,
):
    per, width, order = factor.shape
    near, cross = v_near.shape[1], v_cross.shape[1]
    half = n // 2
    planes = half // 2
    cut = [per * p // parts for p in range(parts + 1)]
    r = lax.axis_index("rows")
    q = lax.axis_index("col")
    upper = r // half
    is_upper = upper == 1
    m = r - upper * half
    s = m % 2
    d = jnp.where(is_upper, m // 2, planes - 1 - m // 2)
    inmost = d == 0
    beyond = d > 0
    lower_inmost = jnp.logical_and(upper == 0, inmost)
    upper_inmost = jnp.logical_and(is_upper, inmost)
    has_outer = d + 1 < planes
    first_core = q % 2 == 0
    mate = r + 1 - 2 * s
    target = jnp.where(is_upper, half - 2 + s, half + s)
    outer = jnp.where(is_upper, r + 2, r - 2)
    col_mate = q + 1 - 2 * (q % 2)
    col_cousins = [(q + 2 * k) % c for k in range(1, c // 2)]
    cousins = len(col_cousins)
    origin = jnp.logical_and(r == 0, q == 0)
    CORE, MATE, NEXT, CROSS, COUSIN = 0, 1, 2, 3, 4

    def other_row(e, side):
        return jnp.where(is_upper, half - 2 - 2 * e, half + 2 * e) + side

    loads = [
        pltpu.make_async_copy(s_diag, v_diag, load_sem.at[0]),
        pltpu.make_async_copy(s_near, v_near, load_sem.at[1]),
        pltpu.make_async_copy(s_cross, v_cross, load_sem.at[2]),
        pltpu.make_async_copy(near_cols, near_at, load_sem.at[3]),
        pltpu.make_async_copy(cross_cols, cross_at, load_sem.at[4]),
    ]

    def beside(step):
        return nearby.at[pl.ds((1 + step) * per, per)]

    own_near = pltpu.make_async_copy(factor, beside(0), own_sem.at[0])

    def rows_of(column):
        return pl.ds(pl.multiple_of(column * width, width), width)

    own_full = pltpu.make_async_copy(factor, full.at[:, rows_of(q), :], own_sem.at[1])

    barrier = pltpu.get_barrier_semaphore()

    def signal(sem, **where):
        pl.semaphore_signal(sem, inc=1, device_id=where, device_id_type=pl.DeviceIdType.MESH)

    greets = [
        (jnp.logical_or(q < col_mate, jnp.logical_and(r == 0, col_mate == 0)), {"col": col_mate}),
        (s == 0, {"rows": mate}),
        (jnp.logical_and(upper == 0, m + 2 < half), {"rows": r + 2}),
        (jnp.logical_and(upper == 0, beyond), {"rows": half + s}),
    ] + [(lower_inmost, {"rows": half + 2 * e + s}) for e in range(planes)]
    greets += [(q < column, {"col": column}) for column in col_cousins]
    late_greets = [(jnp.logical_and(is_upper, m + 2 < half), {"rows": r + 2})]
    heard = [jnp.logical_or(q > col_mate, origin), s == 1, m >= 2, is_upper] + [q > column for column in col_cousins]
    heard += [upper_inmost] * (planes - 1)
    answers = [
        (q > col_mate, CORE, {"col": col_mate}),
        (s == 1, MATE, {"rows": mate}),
        (m >= 2, NEXT, {"rows": r - 2}),
    ] + [(upper_inmost, CROSS, {"rows": half - 2 - 2 * e + s}) for e in range(planes)]
    answers += [(q > column, COUSIN + cousins - 1 - k, {"col": column}) for k, column in enumerate(col_cousins)]

    for condition, where in greets:
        pl.when(condition)(functools.partial(signal, barrier, **where))

    own_full.start()
    own_near.start()
    for load in loads:
        load.start()
    with jax.named_scope("bar"):
        pl.semaphore_wait(barrier, sum(x.astype(jnp.int32) for x in heard))
    for condition, where in late_greets:
        pl.when(condition)(functools.partial(signal, barrier, **where))
    for condition, k, where in answers:
        pl.when(condition)(functools.partial(signal, ready.at[k], **where))

    def send(src, dst, send_sem, recv_sem, **where):
        return pltpu.make_async_remote_copy(
            src_ref=src, dst_ref=dst, send_sem=send_sem, recv_sem=recv_sem,
            device_id=where, device_id_type=pl.DeviceIdType.MESH,
        )

    halves = split(per, col_recv.shape[1])

    def column_piece(column, h):
        return full.at[halves[h], rows_of(column), :]

    def slot(row, p):
        return everyone.at[pl.ds(row * per + cut[p], cut[p + 1] - cut[p])]

    crossing = [
        send(
            factor.at[pl.ds(cut[p], cut[p + 1] - cut[p])], slot(r, p),
            cross_send.at[0], chain_recv.at[d, p], rows=target,
        )
        for p in range(parts)
    ]
    toward = 1 - 2 * s
    to_mate = [send(factor, beside(-toward), near_send.at[0], near_recv.at[0], rows=mate)]
    to_core = [
        send(factor.at[halves[h]], column_piece(q, h), col_send.at[0], col_recv.at[q, h], col=col_mate)
        for h in range(len(halves))
    ]
    to_cousins = [
        [
            send(factor.at[halves[h]], column_piece(q, h), col_send.at[0], col_recv.at[q, h], col=column)
            for h in range(len(halves))
        ]
        for k, column in enumerate(col_cousins)
    ]
    firsts = [(is_upper, None, crossing), (s == 1, MATE, to_mate)]
    firsts += [(q > column, COUSIN + k, to_cousins[k]) for k, column in enumerate(col_cousins)]
    firsts += [(q > col_mate, CORE, to_core)]

    def start_all(copies):
        for copy in copies:
            copy.start()

    with jax.named_scope("own"):
        for condition, _, copies in firsts:
            pl.when(condition)(functools.partial(start_all, copies))

        def after_answer(k, copies):
            pl.semaphore_wait(ready.at[k], 1)
            start_all(copies)

        for condition, k, copies in firsts[:0:-1]:
            pl.when(jnp.logical_not(condition))(functools.partial(after_answer, k, copies))
        pl.when(upper == 0)(functools.partial(after_answer, CROSS, crossing))
        pl.when(m + 2 < half)(lambda: pl.semaphore_wait(ready.at[NEXT], 1))

    sent = [(None, copy) for copy in to_mate]

    def landed(ref, sem):
        send(ref, ref, near_send.at[0], sem, rows=mate).wait_recv()

    def spread(e, p):
        ref = slot(other_row(e, s), p)
        return (
            send(ref, ref, outer_send.at[0], chain_recv.at[e, p], rows=outer),
            send(ref, ref, mate_send.at[0], mate_recv.at[e], rows=mate),
        )

    def forward(e, p):
        landed(slot(other_row(e, s), p), chain_recv.at[e, p])
        on, across = spread(e, p)
        pl.when(has_outer)(on.start)
        across.start()

    slant = jnp.logical_and(jnp.logical_and(lower_inmost, has_outer), s == 1)
    slanted = jnp.logical_and(jnp.logical_and(upper == 0, d == 1), s == 1)

    def forward_last(e, p):
        ref = slot(other_row(e, s), p)
        landed(ref, chain_recv.at[e, p])
        on, across = spread(e, p)
        aslant = send(ref, ref, slant_send.at[0], mate_recv.at[e], rows=outer - 1)
        pl.when(slant)(aslant.start)
        pl.when(jnp.logical_and(has_outer, jnp.logical_not(slant)))(on.start)
        pl.when(jnp.logical_not(slanted))(across.start)

    def near_copy(src_ref, step, row):
        return send(src_ref, beside(step), near_send.at[1], near_recv.at[1], rows=row)

    passing = near_copy(beside(toward), -toward, r + 2 * toward)
    prompt = jnp.logical_and(lower_inmost, first_core)
    passes = jnp.logical_and(jnp.where(s == 1, m >= 2, m + 2 < half), jnp.logical_not(jnp.logical_and(prompt, s == 1)))
    direct = near_copy(factor, 1, r - 1)
    directs = jnp.logical_and(jnp.logical_and(prompt, s == 0), m >= 2)
    sent += [(passes, passing), (directs, direct)]

    def pass_near(where):
        pl.when(jnp.logical_and(where, passes))(passing.start)
        pl.when(jnp.logical_and(where, directs))(direct.start)

    def arrive_column(column, h):
        landed(column_piece(column, h), col_recv.at[column, h])

    eye = (
        lax.broadcasted_iota(jnp.int32, (width, order), 0) + q * width
        == lax.broadcasted_iota(jnp.int32, (width, order), 1)
    ).astype(F32)

    def prepare(i, carry):
        z_t = full[i]
        own = full[i, rows_of(q), :]
        square = (-0.5 * dot(z_t, z_t, TN)).astype(BF16)
        blocks = [v_near[i, k] for k in range(near)] + [v_cross[i, k] for k in range(cross)]
        tall = dot(jnp.concatenate(blocks, axis=1), square, TN).astype(BF16)
        for k in range(near + cross):
            g[i, k] = tall[k * order:(k + 1) * order]
        product = dot(own, v_diag[i], NT).astype(BF16)
        residual = (eye - dot(product, z_t, NT)).astype(BF16)
        w_diag[i] = (own.astype(F32) + 0.5 * dot(residual, z_t)).astype(BF16)
        return carry

    def rows_from(e):
        return everyone.at[pl.ds(other_row(e, 1 - s) * per, per)]

    chunks = [(e, p) for e in range(planes) for p in range(parts)]

    def forwards(first, last):
        for e, p in chunks[first:last]:
            with jax.named_scope(f"x{e}{p}"):
                forward(e, p)

    def pass_columns():
        for h in range(len(halves)):
            for k, column in enumerate(col_cousins):
                arrive_column(column, h)
                ref = column_piece(column, h)
                send(ref, ref, col_send.at[0], col_recv.at[column, h], col=col_mate).start()

    heads = [
        (jnp.logical_and(first_core, upper == 0), 1),
        (jnp.logical_and(first_core, is_upper), 0),
        (jnp.logical_not(first_core), max(1, parts * 3 // 4)),
    ]

    middle = len(chunks) - parts - parts // 2

    def pieces_of(head):
        passing = chunks[parts:]
        return chunks[:head], passing[:middle], passing[middle:], chunks[head:parts]

    def aslant_from(head):
        return 2 if head == 1 else 3

    def take(where, *places):
        for condition, head in heads:
            def some():
                last = []
                for place in places:
                    for e, p in pieces_of(head)[place]:
                        with jax.named_scope(f"x{e}{p}"):
                            if place < aslant_from(head):
                                forward(e, p)
                            else:
                                forward_last(e, p)
                                last.append(spread(e, p)[0])
                if last:
                    pl.when(slant)(functools.partial(start_all, last))
            pl.when(jnp.logical_and(where, condition))(some)

    beyond_first = jnp.logical_and(beyond, first_core)
    beyond_second = jnp.logical_and(beyond, jnp.logical_not(first_core))

    def spread_rows(step, first, last):
        with jax.named_scope(f"prep{step}"):
            lax.fori_loop(first, last, prepare, 0, unroll=True)

    take(inmost, 0)
    with jax.named_scope("colf"):
        pass_columns()
    take(inmost, 1)
    take(beyond_second, 0)
    with jax.named_scope("mate"):
        landed(beside(toward), near_recv.at[0])
    take(inmost, 2, 3)
    pass_near(prompt)
    with jax.named_scope("loads"):
        own_full.wait()
        for load in loads:
            load.wait()
    with jax.named_scope("cols"):
        for h in range(len(halves)):
            arrive_column(col_mate, h)
            for k in range(1, c // 2):
                arrive_column((col_mate + 2 * k) % c, h)

    row_cut = [per * k // 14 for k in ROW_CUT]
    spread_rows(0, row_cut[0], row_cut[1])
    take(beyond_first, 0)
    take(beyond_second, 1, 2)
    with jax.named_scope("near"):
        pass_near(jnp.logical_not(lower_inmost))
    spread_rows(1, row_cut[1], row_cut[2])
    pass_near(jnp.logical_and(lower_inmost, jnp.logical_not(first_core)))
    passes_on = jnp.logical_and(beyond, jnp.logical_not(slanted))
    take(beyond_first, 1)
    take(jnp.logical_and(passes_on, first_core), 2)
    take(passes_on, 3)
    spread_rows(2, row_cut[2], row_cut[3])
    take(jnp.logical_and(slanted, first_core), 2)
    take(slanted, 3)

    with jax.named_scope("nwait"):
        own_near.wait()
        within = jnp.logical_and(m - toward >= 0, m - toward < half)
        edge = jnp.logical_and(jnp.logical_not(within), jnp.logical_and(r - toward >= 0, r - toward < n))
        pl.when(within)(functools.partial(landed, beside(-toward), near_recv.at[1]))

        @pl.when(edge)
        def _():
            landed(rows_from(0), mate_recv.at[0])
            copy = pltpu.make_async_copy(everyone.at[pl.ds((r - toward) * per, per)], beside(-toward), edge_sem.at[0])
            copy.start()
            copy.wait()

    base = (r - 1) * per

    def finish_near(i, carry):
        for k in range(near):
            place = jnp.clip(near_at[k, i] - base, 0, 3 * per - 1)
            w_near[i, k] = dot(nearby[place], g[i, k]).astype(BF16)
        return carry

    def finish_cross(i, carry):
        for k in range(cross):
            w_cross[i, k] = dot(everyone[cross_at[k, i]], g[i, near + k]).astype(BF16)
        return carry

    with jax.named_scope("ndots"):
        lax.fori_loop(0, per, finish_near, 0, unroll=True)
    with jax.named_scope("fin"):
        pl.when(jnp.logical_not(edge))(functools.partial(landed, rows_from(0), mate_recv.at[0]))
        for e in range(1, planes):
            landed(rows_from(e), mate_recv.at[e])
    with jax.named_scope("cdots"):
        lax.fori_loop(0, per, finish_cross, 0, unroll=True)
    with jax.named_scope("sends"):
        def gone(ref, sem):
            send(ref, ref, sem, near_recv.at[0], rows=mate).wait_send()

        pl.when(jnp.logical_not(slanted))(functools.partial(gone, everyone.at[pl.ds(0, planes * per)], mate_send.at[0]))
        for condition, head in heads:
            last = sum(cut[p + 1] - cut[p] for piece in pieces_of(head)[aslant_from(head):] for e, p in piece)
            pl.when(jnp.logical_and(slanted, condition))(
                functools.partial(gone, everyone.at[pl.ds(0, planes * per - last)], mate_send.at[0])
            )
            if last:
                pl.when(jnp.logical_and(slant, condition))(
                    functools.partial(gone, everyone.at[pl.ds(0, last)], slant_send.at[0])
                )
        pl.when(has_outer)(functools.partial(gone, everyone.at[pl.ds(0, planes * per)], outer_send.at[0]))
        gone(everyone.at[pl.ds(0, per)], cross_send.at[0])
        gone(everyone.at[pl.ds(0, per * (2 * cousins + 1))], col_send.at[0])
        for condition, copy in sent:
            if condition is None:
                copy.wait_send()
            else:
                pl.when(condition)(copy.wait_send)


def store_kernel(w_diag, w_near, w_cross, o_diag, o_near, o_cross, sem):
    copies = [
        pltpu.make_async_copy(w_diag, o_diag, sem.at[0]),
        pltpu.make_async_copy(w_near, o_near, sem.at[1]),
        pltpu.make_async_copy(w_cross, o_cross, sem.at[2]),
    ]
    for copy in copies:
        copy.start()
    for copy in copies:
        copy.wait()


def body(n, c, factor_t, intersection_diag, intersection_near, intersection_cross, near_cols, cross_cols):
    per, width, order = factor_t.shape
    near, cross = near_cols.shape[1], cross_cols.shape[1]
    planes = n // 4
    parts = max(1, min(PARTS // planes, per))
    col_parts = 2 if per % 2 == 0 else 1
    smem = pltpu.SMEM
    vmem = pl.BlockSpec(memory_space=pltpu.VMEM)
    hbm = pl.BlockSpec(memory_space=pl.ANY)
    dma = pltpu.SemaphoreType.DMA
    shapes = ((per, width, order), (per, near, width, order), (per, cross, width, order))
    kept = 2 * order * width * per * (1 + near + cross)
    results = pl.pallas_call(
        functools.partial(refine_kernel, n, c, parts),
        out_shape=tuple(pltpu.VMEM(shape, BF16) for shape in shapes),
        in_specs=[pl.BlockSpec(memory_space=pltpu.HBM)] * 6,
        out_specs=(vmem,) * 3,
        scratch_shapes=[
            pltpu.VMEM((n * per, width, order), BF16),
            pltpu.VMEM((3 * per, width, order), BF16),
            pltpu.VMEM((per, near + cross, order, order), BF16),
            pltpu.VMEM((per, order, order), BF16),
            pltpu.VMEM(intersection_diag.shape, BF16),
            pltpu.VMEM(intersection_near.shape, BF16),
            pltpu.VMEM(intersection_cross.shape, BF16),
            smem((near, per), jnp.int32),
            smem((cross, per), jnp.int32),
            dma((5,)),
            dma((2,)),
            dma((1,)),
            dma((1,)),
            dma((c, col_parts)),
            dma((2,)),
            dma((2,)),
            dma((1,)),
            dma((1,)),
            dma((1,)),
            dma((1,)),
            dma((planes, parts)),
            dma((planes,)),
            pltpu.SemaphoreType.REGULAR((3 + c // 2,)),
        ],
        compiler_params=pltpu.CompilerParams(
            collective_id=0, has_side_effects=True, vmem_limit_bytes=VMEM_ALL - kept - SLACK,
        ),
    )(factor_t, intersection_diag, intersection_near, intersection_cross, near_cols.T, cross_cols.T)
    return pl.pallas_call(
        store_kernel,
        out_shape=tuple(jax.ShapeDtypeStruct(shape, BF16) for shape in shapes),
        in_specs=[vmem] * 3,
        out_specs=(hbm,) * 3,
        scratch_shapes=[dma((3,))],
        compiler_params=pltpu.CompilerParams(vmem_limit_bytes=VMEM_LIMIT),
    )(*results)


def solution(mesh):
    placed = (
        P("rows", "col", None),
        P("rows", None, None),
        P("rows", None, None, None),
        P("rows", None, None, None),
        P("rows", None),
        P("rows", None),
    )
    return jax.shard_map(
        functools.partial(body, mesh.shape["rows"], mesh.shape["col"]),
        mesh=mesh,
        in_specs=placed,
        out_specs=(
            P("rows", "col", None),
            P("rows", None, "col", None),
            P("rows", None, "col", None),
        ),
        check_vma=False,
    )
```

```python
import functools

import jax
import jax.numpy as jnp
from jax import lax
from jax.experimental import pallas as pl
from jax.experimental.pallas import tpu as pltpu
from jax.sharding import PartitionSpec as P

F32 = jnp.float32
BF16 = jnp.bfloat16
PARTS = 14
ROW_CUT = (0, 5, 10, 14)
VMEM_LIMIT = 16 * 1024 * 1024
VMEM_ALL = 67043328
SLACK = 96 * 1024
NT = (((1,), (1,)), ((), ()))
TN = (((0,), (0,)), ((), ()))


def dot(a, b, dims=(((1,), (0,)), ((), ()))):
    return lax.dot_general(a, b, dims, preferred_element_type=F32)


def split(rows, parts):
    size = rows // parts
    return [pl.ds(p * size, size) for p in range(parts)]


def refine_kernel(
    n, c, parts,
    factor, s_diag, s_near, s_cross, near_cols, cross_cols,
    w_diag, w_near, w_cross,
    everyone, nearby, g, full, v_diag, v_near, v_cross, near_at, cross_at,
    load_sem, own_sem, edge_sem, col_send, col_recv, near_send, near_recv,
    cross_send, outer_send, mate_send, slant_send, chain_recv, mate_recv, ready,
):
    per, width, order = factor.shape
    near, cross = v_near.shape[1], v_cross.shape[1]
    half = n // 2
    planes = half // 2
    cut = [per * p // parts for p in range(parts + 1)]
    r = lax.axis_index("rows")
    q = lax.axis_index("col")
    upper = r // half
    is_upper = upper == 1
    m = r - upper * half
    s = m % 2
    d = jnp.where(is_upper, m // 2, planes - 1 - m // 2)
    inmost = d == 0
    beyond = d > 0
    lower_inmost = jnp.logical_and(upper == 0, inmost)
    upper_inmost = jnp.logical_and(is_upper, inmost)
    has_outer = d + 1 < planes
    first_core = q % 2 == 0
    mate = r + 1 - 2 * s
    target = jnp.where(is_upper, half - 2 + s, half + s)
    outer = jnp.where(is_upper, r + 2, r - 2)
    col_mate = q + 1 - 2 * (q % 2)
    col_cousins = [(q + 2 * k) % c for k in range(1, c // 2)]
    cousins = len(col_cousins)
    origin = jnp.logical_and(r == 0, q == 0)
    CORE, MATE, NEXT, CROSS, SLANT, COUSIN = 0, 1, 2, 3, 4, 5

    def other_row(e, side):
        return jnp.where(is_upper, half - 2 - 2 * e, half + 2 * e) + side

    loads = [
        pltpu.make_async_copy(s_diag, v_diag, load_sem.at[0]),
        pltpu.make_async_copy(s_near, v_near, load_sem.at[1]),
        pltpu.make_async_copy(s_cross, v_cross, load_sem.at[2]),
        pltpu.make_async_copy(near_cols, near_at, load_sem.at[3]),
        pltpu.make_async_copy(cross_cols, cross_at, load_sem.at[4]),
    ]

    def beside(step):
        return nearby.at[pl.ds((1 + step) * per, per)]

    own_near = pltpu.make_async_copy(factor, beside(0), own_sem.at[0])

    def rows_of(column):
        return pl.ds(pl.multiple_of(column * width, width), width)

    own_full = pltpu.make_async_copy(factor, full.at[:, rows_of(q), :], own_sem.at[1])

    barrier = pltpu.get_barrier_semaphore()

    def signal(sem, **where):
        pl.semaphore_signal(sem, inc=1, device_id=where, device_id_type=pl.DeviceIdType.MESH)

    greets = [
        (jnp.logical_or(q < col_mate, jnp.logical_and(r == 0, col_mate == 0)), {"col": col_mate}),
        (s == 0, {"rows": mate}),
        (jnp.logical_and(upper == 0, m + 2 < half), {"rows": r + 2}),
        (jnp.logical_and(upper == 0, beyond), {"rows": half + s}),
    ] + [(lower_inmost, {"rows": half + 2 * e + s}) for e in range(planes)]
    greets += [(q < column, {"col": column}) for column in col_cousins]
    late_greets = [(jnp.logical_and(is_upper, m + 2 < half), {"rows": r + 2})]
    heard = [jnp.logical_or(q > col_mate, origin), s == 1, m >= 2, is_upper] + [q > column for column in col_cousins]
    heard += [upper_inmost] * (planes - 1)
    answers = [
        (q > col_mate, CORE, {"col": col_mate}),
        (s == 1, MATE, {"rows": mate}),
        (m >= 2, NEXT, {"rows": r - 2}),
    ] + [(upper_inmost, CROSS, {"rows": half - 2 - 2 * e + s}) for e in range(planes)]
    answers += [(q > column, COUSIN + cousins - 1 - k, {"col": column}) for k, column in enumerate(col_cousins)]

    for condition, where in greets:
        pl.when(condition)(functools.partial(signal, barrier, **where))

    own_full.start()
    own_near.start()
    for load in loads:
        load.start()
    with jax.named_scope("bar"):
        pl.semaphore_wait(barrier, sum(x.astype(jnp.int32) for x in heard))
    for condition, where in late_greets:
        pl.when(condition)(functools.partial(signal, barrier, **where))
    for condition, k, where in answers:
        pl.when(condition)(functools.partial(signal, ready.at[k], **where))

    def send(src, dst, send_sem, recv_sem, **where):
        return pltpu.make_async_remote_copy(
            src_ref=src, dst_ref=dst, send_sem=send_sem, recv_sem=recv_sem,
            device_id=where, device_id_type=pl.DeviceIdType.MESH,
        )

    halves = split(per, col_recv.shape[1])

    def column_piece(column, h):
        return full.at[halves[h], rows_of(column), :]

    def slot(row, p):
        return everyone.at[pl.ds(row * per + cut[p], cut[p + 1] - cut[p])]

    crossing = [
        send(
            factor.at[pl.ds(cut[p], cut[p + 1] - cut[p])], slot(r, p),
            cross_send.at[0], chain_recv.at[d, p], rows=target,
        )
        for p in range(parts)
    ]
    toward = 1 - 2 * s
    to_mate = [send(factor, beside(-toward), near_send.at[0], near_recv.at[0], rows=mate)]
    to_core = [
        send(factor.at[halves[h]], column_piece(q, h), col_send.at[0], col_recv.at[q, h], col=col_mate)
        for h in range(len(halves))
    ]
    to_cousins = [
        [
            send(factor.at[halves[h]], column_piece(q, h), col_send.at[0], col_recv.at[q, h], col=column)
            for h in range(len(halves))
        ]
        for k, column in enumerate(col_cousins)
    ]
    firsts = [(is_upper, None, crossing), (s == 1, MATE, to_mate)]
    firsts += [(q > column, COUSIN + k, to_cousins[k]) for k, column in enumerate(col_cousins)]
    firsts += [(q > col_mate, CORE, to_core)]

    def start_all(copies):
        for copy in copies:
            copy.start()

    with jax.named_scope("own"):
        for condition, _, copies in firsts:
            pl.when(condition)(functools.partial(start_all, copies))

        def after_answer(k, copies):
            pl.semaphore_wait(ready.at[k], 1)
            start_all(copies)

        for condition, k, copies in firsts[:0:-1]:
            pl.when(jnp.logical_not(condition))(functools.partial(after_answer, k, copies))
        pl.when(jnp.logical_and(jnp.logical_and(lower_inmost, has_outer), s == 0))(
            functools.partial(signal, ready.at[SLANT], rows=mate)
        )
        pl.when(upper == 0)(functools.partial(after_answer, CROSS, crossing))
        pl.when(m + 2 < half)(lambda: pl.semaphore_wait(ready.at[NEXT], 1))

    sent = [(None, copy) for copy in to_mate]

    def landed(ref, sem):
        send(ref, ref, near_send.at[0], sem, rows=mate).wait_recv()

    def spread(e, p):
        ref = slot(other_row(e, s), p)
        return (
            send(ref, ref, outer_send.at[0], chain_recv.at[e, p], rows=outer),
            send(ref, ref, mate_send.at[0], mate_recv.at[e], rows=mate),
        )

    def forward(e, p):
        landed(slot(other_row(e, s), p), chain_recv.at[e, p])
        on, across = spread(e, p)
        pl.when(has_outer)(on.start)
        across.start()

    slant = jnp.logical_and(jnp.logical_and(lower_inmost, has_outer), s == 1)
    slanted = jnp.logical_and(jnp.logical_and(upper == 0, d == 1), s == 1)

    def forward_last(e, p):
        ref = slot(other_row(e, s), p)
        landed(ref, chain_recv.at[e, p])
        on, across = spread(e, p)
        aslant = send(ref, ref, slant_send.at[0], mate_recv.at[e], rows=outer - 1)
        pl.when(slant)(aslant.start)
        pl.when(jnp.logical_and(has_outer, jnp.logical_not(slant)))(on.start)
        pl.when(jnp.logical_not(slanted))(across.start)

    def near_copy(src_ref, step, row):
        return send(src_ref, beside(step), near_send.at[1], near_recv.at[1], rows=row)

    passing = near_copy(beside(toward), -toward, r + 2 * toward)
    prompt = jnp.logical_and(lower_inmost, first_core)
    passes = jnp.logical_and(jnp.where(s == 1, m >= 2, m + 2 < half), jnp.logical_not(jnp.logical_and(prompt, s == 1)))
    direct = near_copy(factor, 1, r - 1)
    directs = jnp.logical_and(jnp.logical_and(prompt, s == 0), m >= 2)
    sent += [(passes, passing), (directs, direct)]

    def pass_near(where):
        pl.when(jnp.logical_and(where, passes))(passing.start)
        pl.when(jnp.logical_and(where, directs))(direct.start)

    def arrive_column(column, h):
        landed(column_piece(column, h), col_recv.at[column, h])

    eye = (
        lax.broadcasted_iota(jnp.int32, (width, order), 0) + q * width
        == lax.broadcasted_iota(jnp.int32, (width, order), 1)
    ).astype(F32)

    def prepare(i, carry):
        z_t = full[i]
        own = full[i, rows_of(q), :]
        square = (-0.5 * dot(z_t, z_t, TN)).astype(BF16)
        blocks = [v_near[i, k] for k in range(near)] + [v_cross[i, k] for k in range(cross)]
        tall = dot(jnp.concatenate(blocks, axis=1), square, TN).astype(BF16)
        for k in range(near + cross):
            g[i, k] = tall[k * order:(k + 1) * order]
        product = dot(own, v_diag[i], NT).astype(BF16)
        residual = (eye - dot(product, z_t, NT)).astype(BF16)
        w_diag[i] = (own.astype(F32) + 0.5 * dot(residual, z_t)).astype(BF16)
        return carry

    def rows_from(e):
        return everyone.at[pl.ds(other_row(e, 1 - s) * per, per)]

    chunks = [(e, p) for e in range(planes) for p in range(parts)]

    def forwards(first, last):
        for e, p in chunks[first:last]:
            with jax.named_scope(f"x{e}{p}"):
                forward(e, p)

    def pass_columns():
        for h in range(len(halves)):
            for k, column in enumerate(col_cousins):
                arrive_column(column, h)
                ref = column_piece(column, h)
                send(ref, ref, col_send.at[0], col_recv.at[column, h], col=col_mate).start()

    heads = [
        (jnp.logical_and(first_core, upper == 0), 1),
        (jnp.logical_and(first_core, is_upper), 0),
        (jnp.logical_not(first_core), max(1, parts * 3 // 4)),
    ]

    middle = len(chunks) - parts - (parts * 3 // 4)

    def pieces_of(head):
        passing = chunks[parts:]
        return chunks[:head], passing[:middle], passing[middle:], chunks[head:parts]

    def aslant_from(head):
        return 2 if head == 1 else 3

    def take(where, *places):
        for condition, head in heads:
            def some():
                last = []
                for place in places:
                    for e, p in pieces_of(head)[place]:
                        with jax.named_scope(f"x{e}{p}"):
                            if place < aslant_from(head):
                                forward(e, p)
                            else:
                                forward_last(e, p)
                                last.append(spread(e, p)[0])
                if last:
                    pl.when(slant)(functools.partial(start_all, last))
            pl.when(jnp.logical_and(where, condition))(some)

    beyond_first = jnp.logical_and(beyond, first_core)
    beyond_second = jnp.logical_and(beyond, jnp.logical_not(first_core))

    def spread_rows(step, first, last):
        with jax.named_scope(f"prep{step}"):
            lax.fori_loop(first, last, prepare, 0, unroll=True)

    take(inmost, 0)
    with jax.named_scope("colf"):
        pass_columns()
    take(inmost, 1)
    take(beyond_second, 0)
    pl.when(slant)(lambda: pl.semaphore_wait(ready.at[SLANT], 1))
    take(inmost, 2, 3)
    pass_near(prompt)
    with jax.named_scope("loads"):
        own_full.wait()
        for load in loads:
            load.wait()
    with jax.named_scope("cols"):
        for h in range(len(halves)):
            arrive_column(col_mate, h)
            for k in range(1, c // 2):
                arrive_column((col_mate + 2 * k) % c, h)

    row_cut = [per * k // 14 for k in ROW_CUT]
    spread_rows(0, row_cut[0], row_cut[1])
    take(beyond_first, 0)
    take(beyond_second, 1, 2)
    with jax.named_scope("near"):
        landed(beside(toward), near_recv.at[0])
        pass_near(jnp.logical_not(prompt))
    spread_rows(1, row_cut[1], row_cut[2])
    passes_on = jnp.logical_and(beyond, jnp.logical_not(slanted))
    take(beyond_first, 1)
    take(jnp.logical_and(passes_on, first_core), 2)
    take(passes_on, 3)
    spread_rows(2, row_cut[2], row_cut[3])

    with jax.named_scope("nwait"):
        own_near.wait()
        within = jnp.logical_and(m - toward >= 0, m - toward < half)
        edge = jnp.logical_and(jnp.logical_not(within), jnp.logical_and(r - toward >= 0, r - toward < n))
        pl.when(within)(functools.partial(landed, beside(-toward), near_recv.at[1]))

        @pl.when(edge)
        def _():
            landed(rows_from(0), mate_recv.at[0])
            copy = pltpu.make_async_copy(everyone.at[pl.ds((r - toward) * per, per)], beside(-toward), edge_sem.at[0])
            copy.start()
            copy.wait()

    base = (r - 1) * per

    def finish_near(i, carry):
        for k in range(near):
            place = jnp.clip(near_at[k, i] - base, 0, 3 * per - 1)
            w_near[i, k] = dot(nearby[place], g[i, k]).astype(BF16)
        return carry

    def finish_cross(i, carry):
        for k in range(cross):
            w_cross[i, k] = dot(everyone[cross_at[k, i]], g[i, near + k]).astype(BF16)
        return carry

    with jax.named_scope("ndots"):
        lax.fori_loop(0, per, finish_near, 0, unroll=True)
    take(jnp.logical_and(slanted, first_core), 2)
    take(slanted, 3)
    with jax.named_scope("fin"):
        pl.when(jnp.logical_not(edge))(functools.partial(landed, rows_from(0), mate_recv.at[0]))
        for e in range(1, planes):
            landed(rows_from(e), mate_recv.at[e])
    with jax.named_scope("cdots"):
        lax.fori_loop(0, per, finish_cross, 0, unroll=True)
    with jax.named_scope("sends"):
        def gone(ref, sem):
            send(ref, ref, sem, near_recv.at[0], rows=mate).wait_send()

        pl.when(jnp.logical_not(slanted))(functools.partial(gone, everyone.at[pl.ds(0, planes * per)], mate_send.at[0]))
        for condition, head in heads:
            last = sum(cut[p + 1] - cut[p] for piece in pieces_of(head)[aslant_from(head):] for e, p in piece)
            pl.when(jnp.logical_and(slanted, condition))(
                functools.partial(gone, everyone.at[pl.ds(0, planes * per - last)], mate_send.at[0])
            )
            if last:
                pl.when(jnp.logical_and(slant, condition))(
                    functools.partial(gone, everyone.at[pl.ds(0, last)], slant_send.at[0])
                )
        pl.when(has_outer)(functools.partial(gone, everyone.at[pl.ds(0, planes * per)], outer_send.at[0]))
        gone(everyone.at[pl.ds(0, per)], cross_send.at[0])
        gone(everyone.at[pl.ds(0, per * (2 * cousins + 1))], col_send.at[0])
        for condition, copy in sent:
            if condition is None:
                copy.wait_send()
            else:
                pl.when(condition)(copy.wait_send)


def store_kernel(w_diag, w_near, w_cross, o_diag, o_near, o_cross, sem):
    copies = [
        pltpu.make_async_copy(w_diag, o_diag, sem.at[0]),
        pltpu.make_async_copy(w_near, o_near, sem.at[1]),
        pltpu.make_async_copy(w_cross, o_cross, sem.at[2]),
    ]
    for copy in copies:
        copy.start()
    for copy in copies:
        copy.wait()


def body(n, c, factor_t, intersection_diag, intersection_near, intersection_cross, near_cols, cross_cols):
    per, width, order = factor_t.shape
    near, cross = near_cols.shape[1], cross_cols.shape[1]
    planes = n // 4
    parts = max(1, min(PARTS // planes, per))
    col_parts = 2 if per % 2 == 0 else 1
    smem = pltpu.SMEM
    vmem = pl.BlockSpec(memory_space=pltpu.VMEM)
    hbm = pl.BlockSpec(memory_space=pl.ANY)
    dma = pltpu.SemaphoreType.DMA
    shapes = ((per, width, order), (per, near, width, order), (per, cross, width, order))
    kept = 2 * order * width * per * (1 + near + cross)
    results = pl.pallas_call(
        functools.partial(refine_kernel, n, c, parts),
        out_shape=tuple(pltpu.VMEM(shape, BF16) for shape in shapes),
        in_specs=[pl.BlockSpec(memory_space=pltpu.HBM)] * 6,
        out_specs=(vmem,) * 3,
        scratch_shapes=[
            pltpu.VMEM((n * per, width, order), BF16),
            pltpu.VMEM((3 * per, width, order), BF16),
            pltpu.VMEM((per, near + cross, order, order), BF16),
            pltpu.VMEM((per, order, order), BF16),
            pltpu.VMEM(intersection_diag.shape, BF16),
            pltpu.VMEM(intersection_near.shape, BF16),
            pltpu.VMEM(intersection_cross.shape, BF16),
            smem((near, per), jnp.int32),
            smem((cross, per), jnp.int32),
            dma((5,)),
            dma((2,)),
            dma((1,)),
            dma((1,)),
            dma((c, col_parts)),
            dma((2,)),
            dma((2,)),
            dma((1,)),
            dma((1,)),
            dma((1,)),
            dma((1,)),
            dma((planes, parts)),
            dma((planes,)),
            pltpu.SemaphoreType.REGULAR((4 + c // 2,)),
        ],
        compiler_params=pltpu.CompilerParams(
            collective_id=0, has_side_effects=True, vmem_limit_bytes=VMEM_ALL - kept - SLACK,
        ),
    )(factor_t, intersection_diag, intersection_near, intersection_cross, near_cols.T, cross_cols.T)
    return pl.pallas_call(
        store_kernel,
        out_shape=tuple(jax.ShapeDtypeStruct(shape, BF16) for shape in shapes),
        in_specs=[vmem] * 3,
        out_specs=(hbm,) * 3,
        scratch_shapes=[dma((3,))],
        compiler_params=pltpu.CompilerParams(vmem_limit_bytes=VMEM_LIMIT),
    )(*results)


def solution(mesh):
    placed = (
        P("rows", "col", None),
        P("rows", None, None),
        P("rows", None, None, None),
        P("rows", None, None, None),
        P("rows", None),
        P("rows", None),
    )
    return jax.shard_map(
        functools.partial(body, mesh.shape["rows"], mesh.shape["col"]),
        mesh=mesh,
        in_specs=placed,
        out_specs=(
            P("rows", "col", None),
            P("rows", None, "col", None),
            P("rows", None, "col", None),
        ),
        check_vma=False,
    )
```

```python
import functools

import jax
import jax.numpy as jnp
from jax import lax
from jax.experimental import pallas as pl
from jax.experimental.pallas import tpu as pltpu
from jax.sharding import PartitionSpec as P

F32 = jnp.float32
BF16 = jnp.bfloat16
PARTS = 14
ROW_CUT = (0, 5, 10, 14)
VMEM_LIMIT = 16 * 1024 * 1024
VMEM_ALL = 67043328
SLACK = 96 * 1024
NT = (((1,), (1,)), ((), ()))
TN = (((0,), (0,)), ((), ()))


def dot(a, b, dims=(((1,), (0,)), ((), ()))):
    return lax.dot_general(a, b, dims, preferred_element_type=F32)


def split(rows, parts):
    size = rows // parts
    return [pl.ds(p * size, size) for p in range(parts)]


def refine_kernel(
    n, c, parts,
    factor, s_diag, s_near, s_cross, near_cols, cross_cols,
    w_diag, w_near, w_cross,
    everyone, nearby, g, full, v_diag, v_near, v_cross, near_at, cross_at,
    load_sem, own_sem, col_send, col_recv, near_send, near_recv,
    cross_send, outer_send, mate_send, slant_send, chain_recv, mate_recv, ready,
):
    per, width, order = factor.shape
    near, cross = v_near.shape[1], v_cross.shape[1]
    half = n // 2
    planes = half // 2
    cut = [per * p // parts for p in range(parts + 1)]
    r = lax.axis_index("rows")
    q = lax.axis_index("col")
    upper = r // half
    is_upper = upper == 1
    m = r - upper * half
    s = m % 2
    d = jnp.where(is_upper, m // 2, planes - 1 - m // 2)
    inmost = d == 0
    beyond = d > 0
    lower_inmost = jnp.logical_and(upper == 0, inmost)
    upper_inmost = jnp.logical_and(is_upper, inmost)
    has_outer = d + 1 < planes
    first_core = q % 2 == 0
    mate = r + 1 - 2 * s
    target = jnp.where(is_upper, half - 2 + s, half + s)
    outer = jnp.where(is_upper, r + 2, r - 2)
    col_mate = q + 1 - 2 * (q % 2)
    col_cousins = [(q + 2 * k) % c for k in range(1, c // 2)]
    cousins = len(col_cousins)
    origin = jnp.logical_and(r == 0, q == 0)
    CORE, MATE, NEXT, CROSS, SLANT, COUSIN = 0, 1, 2, 3, 4, 5

    def other_row(e, side):
        return jnp.where(is_upper, half - 2 - 2 * e, half + 2 * e) + side

    loads = [
        pltpu.make_async_copy(s_diag, v_diag, load_sem.at[0]),
        pltpu.make_async_copy(s_near, v_near, load_sem.at[1]),
        pltpu.make_async_copy(s_cross, v_cross, load_sem.at[2]),
        pltpu.make_async_copy(near_cols, near_at, load_sem.at[3]),
        pltpu.make_async_copy(cross_cols, cross_at, load_sem.at[4]),
    ]

    def beside(step):
        return nearby.at[pl.ds((1 + step) * per, per)]

    own_near = pltpu.make_async_copy(factor, beside(0), own_sem.at[0])

    def rows_of(column):
        return pl.ds(pl.multiple_of(column * width, width), width)

    own_full = pltpu.make_async_copy(factor, full.at[:, rows_of(q), :], own_sem.at[1])

    barrier = pltpu.get_barrier_semaphore()

    def signal(sem, **where):
        pl.semaphore_signal(sem, inc=1, device_id=where, device_id_type=pl.DeviceIdType.MESH)

    greets = [
        (jnp.logical_or(q < col_mate, jnp.logical_and(r == 0, col_mate == 0)), {"col": col_mate}),
        (s == 0, {"rows": mate}),
        (jnp.logical_and(upper == 0, m + 2 < half), {"rows": r + 2}),
        (jnp.logical_and(upper == 0, beyond), {"rows": half + s}),
    ] + [(lower_inmost, {"rows": half + 2 * e + s}) for e in range(planes)]
    greets += [(q < column, {"col": column}) for column in col_cousins]
    late_greets = [(jnp.logical_and(is_upper, m + 2 < half), {"rows": r + 2})]
    heard = [jnp.logical_or(q > col_mate, origin), s == 1, m >= 2, is_upper] + [q > column for column in col_cousins]
    heard += [upper_inmost] * (planes - 1)
    answers = [
        (q > col_mate, CORE, {"col": col_mate}),
        (s == 1, MATE, {"rows": mate}),
        (m >= 2, NEXT, {"rows": r - 2}),
    ] + [(upper_inmost, CROSS, {"rows": half - 2 - 2 * e + s}) for e in range(planes)]
    answers += [(q > column, COUSIN + cousins - 1 - k, {"col": column}) for k, column in enumerate(col_cousins)]

    for condition, where in greets:
        pl.when(condition)(functools.partial(signal, barrier, **where))

    own_full.start()
    own_near.start()
    for load in loads:
        load.start()
    with jax.named_scope("bar"):
        pl.semaphore_wait(barrier, sum(x.astype(jnp.int32) for x in heard))
    for condition, where in late_greets:
        pl.when(condition)(functools.partial(signal, barrier, **where))
    for condition, k, where in answers:
        pl.when(condition)(functools.partial(signal, ready.at[k], **where))

    def send(src, dst, send_sem, recv_sem, **where):
        return pltpu.make_async_remote_copy(
            src_ref=src, dst_ref=dst, send_sem=send_sem, recv_sem=recv_sem,
            device_id=where, device_id_type=pl.DeviceIdType.MESH,
        )

    halves = split(per, col_recv.shape[1])

    def column_piece(column, h):
        return full.at[halves[h], rows_of(column), :]

    def slot(row, p):
        return everyone.at[pl.ds(row * per + cut[p], cut[p + 1] - cut[p])]

    crossing = [
        send(
            factor.at[pl.ds(cut[p], cut[p + 1] - cut[p])], slot(r, p),
            cross_send.at[0], chain_recv.at[d, p], rows=target,
        )
        for p in range(parts)
    ]
    toward = 1 - 2 * s
    to_mate = [send(factor, beside(-toward), near_send.at[0], near_recv.at[0], rows=mate)]
    to_core = [
        send(factor.at[halves[h]], column_piece(q, h), col_send.at[0], col_recv.at[q, h], col=col_mate)
        for h in range(len(halves))
    ]
    to_cousins = [
        [
            send(factor.at[halves[h]], column_piece(q, h), col_send.at[0], col_recv.at[q, h], col=column)
            for h in range(len(halves))
        ]
        for k, column in enumerate(col_cousins)
    ]
    firsts = [(is_upper, None, crossing), (s == 1, MATE, to_mate)]
    firsts += [(q > column, COUSIN + k, to_cousins[k]) for k, column in enumerate(col_cousins)]
    firsts += [(q > col_mate, CORE, to_core)]

    def start_all(copies):
        for copy in copies:
            copy.start()

    with jax.named_scope("own"):
        for condition, _, copies in firsts:
            pl.when(condition)(functools.partial(start_all, copies))

        def after_answer(k, copies):
            pl.semaphore_wait(ready.at[k], 1)
            start_all(copies)

        for condition, k, copies in firsts[:0:-1]:
            pl.when(jnp.logical_not(condition))(functools.partial(after_answer, k, copies))
        pl.when(jnp.logical_and(jnp.logical_and(lower_inmost, has_outer), s == 0))(
            functools.partial(signal, ready.at[SLANT], rows=mate)
        )
        pl.when(upper == 0)(functools.partial(after_answer, CROSS, crossing))
        pl.when(m + 2 < half)(lambda: pl.semaphore_wait(ready.at[NEXT], 1))

    sent = [(None, copy) for copy in to_mate]

    def landed(ref, sem):
        send(ref, ref, near_send.at[0], sem, rows=mate).wait_recv()

    def spread(e, p):
        ref = slot(other_row(e, s), p)
        return (
            send(ref, ref, outer_send.at[0], chain_recv.at[e, p], rows=outer),
            send(ref, ref, mate_send.at[0], mate_recv.at[e], rows=mate),
        )

    def forward(e, p):
        landed(slot(other_row(e, s), p), chain_recv.at[e, p])
        on, across = spread(e, p)
        pl.when(has_outer)(on.start)
        across.start()

    slant = jnp.logical_and(jnp.logical_and(lower_inmost, has_outer), s == 1)
    slanted = jnp.logical_and(jnp.logical_and(upper == 0, d == 1), s == 1)

    def forward_last(e, p):
        ref = slot(other_row(e, s), p)
        landed(ref, chain_recv.at[e, p])
        on, across = spread(e, p)
        aslant = send(ref, ref, slant_send.at[0], mate_recv.at[e], rows=outer - 1)
        pl.when(slant)(aslant.start)
        pl.when(jnp.logical_and(has_outer, jnp.logical_not(slant)))(on.start)
        pl.when(jnp.logical_not(slanted))(across.start)

    def near_copy(src_ref, step, row):
        return send(src_ref, beside(step), near_send.at[1], near_recv.at[1], rows=row)

    passing = near_copy(beside(toward), -toward, r + 2 * toward)
    prompt = jnp.logical_and(lower_inmost, first_core)
    passes = jnp.logical_and(jnp.where(s == 1, m >= 2, m + 2 < half), jnp.logical_not(jnp.logical_and(prompt, s == 1)))
    direct = near_copy(factor, 1, r - 1)
    directs = jnp.logical_and(jnp.logical_and(prompt, s == 0), m >= 2)
    sent += [(passes, passing), (directs, direct)]

    def pass_near(where):
        pl.when(jnp.logical_and(where, passes))(passing.start)
        pl.when(jnp.logical_and(where, directs))(direct.start)

    def arrive_column(column, h):
        landed(column_piece(column, h), col_recv.at[column, h])

    eye = (
        lax.broadcasted_iota(jnp.int32, (width, order), 0) + q * width
        == lax.broadcasted_iota(jnp.int32, (width, order), 1)
    ).astype(F32)

    def prepare(i, carry):
        z_t = full[i]
        own = full[i, rows_of(q), :]
        square = (-0.5 * dot(z_t, z_t, TN)).astype(BF16)
        blocks = [v_near[i, k] for k in range(near)] + [v_cross[i, k] for k in range(cross)]
        tall = dot(jnp.concatenate(blocks, axis=1), square, TN).astype(BF16)
        for k in range(near + cross):
            g[i, k] = tall[k * order:(k + 1) * order]
        product = dot(own, v_diag[i], NT).astype(BF16)
        residual = (eye - dot(product, z_t, NT)).astype(BF16)
        w_diag[i] = (own.astype(F32) + 0.5 * dot(residual, z_t)).astype(BF16)
        return carry

    def rows_from(e):
        return everyone.at[pl.ds(other_row(e, 1 - s) * per, per)]

    chunks = [(e, p) for e in range(planes) for p in range(parts)]

    def forwards(first, last):
        for e, p in chunks[first:last]:
            with jax.named_scope(f"x{e}{p}"):
                forward(e, p)

    def pass_columns():
        for h in range(len(halves)):
            for k, column in enumerate(col_cousins):
                arrive_column(column, h)
                ref = column_piece(column, h)
                send(ref, ref, col_send.at[0], col_recv.at[column, h], col=col_mate).start()

    heads = [
        (jnp.logical_and(first_core, upper == 0), 1),
        (jnp.logical_and(first_core, is_upper), 0),
        (jnp.logical_not(first_core), max(1, parts * 3 // 4)),
    ]

    middle = len(chunks) - parts - (parts * 3 // 4)

    def pieces_of(head):
        passing = chunks[parts:]
        return chunks[:head], passing[:middle], passing[middle:], chunks[head:parts]

    def aslant_from(head):
        return 2 if head == 1 else 3

    def take(where, *places):
        for condition, head in heads:
            def some():
                last = []
                for place in places:
                    for e, p in pieces_of(head)[place]:
                        with jax.named_scope(f"x{e}{p}"):
                            if place < aslant_from(head):
                                forward(e, p)
                            else:
                                forward_last(e, p)
                                last.append(spread(e, p)[0])
                if last:
                    pl.when(slant)(functools.partial(start_all, last))
            pl.when(jnp.logical_and(where, condition))(some)

    beyond_first = jnp.logical_and(beyond, first_core)
    beyond_second = jnp.logical_and(beyond, jnp.logical_not(first_core))

    def spread_rows(step, first, last):
        with jax.named_scope(f"prep{step}"):
            lax.fori_loop(first, last, prepare, 0, unroll=True)

    take(inmost, 0)
    with jax.named_scope("colf"):
        pass_columns()
    take(inmost, 1)
    take(beyond_second, 0)
    pl.when(slant)(lambda: pl.semaphore_wait(ready.at[SLANT], 1))
    take(inmost, 2, 3)
    pass_near(prompt)
    with jax.named_scope("loads"):
        own_full.wait()
        for load in loads:
            load.wait()
    with jax.named_scope("cols"):
        for h in range(len(halves)):
            arrive_column(col_mate, h)
            for k in range(1, c // 2):
                arrive_column((col_mate + 2 * k) % c, h)

    row_cut = [per * k // 14 for k in ROW_CUT]
    spread_rows(0, row_cut[0], row_cut[1])
    take(beyond_first, 0)
    take(beyond_second, 1, 2)
    with jax.named_scope("near"):
        landed(beside(toward), near_recv.at[0])
        pass_near(jnp.logical_not(prompt))
    spread_rows(1, row_cut[1], row_cut[2])
    passes_on = jnp.logical_and(beyond, jnp.logical_not(slanted))
    take(beyond_first, 1)
    take(jnp.logical_and(passes_on, first_core), 2)
    take(passes_on, 3)
    spread_rows(2, row_cut[2], row_cut[3])

    with jax.named_scope("nwait"):
        own_near.wait()
        within = jnp.logical_and(m - toward >= 0, m - toward < half)
        edge = jnp.logical_and(jnp.logical_not(within), jnp.logical_and(r - toward >= 0, r - toward < n))
        pl.when(within)(functools.partial(landed, beside(-toward), near_recv.at[1]))

        @pl.when(edge)
        def _():
            landed(rows_from(0), mate_recv.at[0])
            copy = pltpu.make_async_copy(everyone.at[pl.ds((r - toward) * per, per)], beside(-toward), own_sem.at[0])
            copy.start()
            copy.wait()

    base = (r - 1) * per

    def finish_near(i, carry):
        for k in range(near):
            place = jnp.clip(near_at[k, i] - base, 0, 3 * per - 1)
            w_near[i, k] = dot(nearby[place], g[i, k]).astype(BF16)
        return carry

    def finish_cross(i, carry):
        for k in range(cross):
            w_cross[i, k] = dot(everyone[cross_at[k, i]], g[i, near + k]).astype(BF16)
        return carry

    with jax.named_scope("ndots"):
        lax.fori_loop(0, per, finish_near, 0, unroll=True)
    take(jnp.logical_and(slanted, first_core), 2)
    take(slanted, 3)
    with jax.named_scope("fin"):
        pl.when(jnp.logical_not(edge))(functools.partial(landed, rows_from(0), mate_recv.at[0]))
        for e in range(1, planes):
            landed(rows_from(e), mate_recv.at[e])
    with jax.named_scope("cdots"):
        lax.fori_loop(0, per, finish_cross, 0, unroll=True)
    with jax.named_scope("sends"):
        def gone(ref, sem):
            send(ref, ref, sem, near_recv.at[0], rows=mate).wait_send()

        pl.when(jnp.logical_not(slanted))(functools.partial(gone, everyone.at[pl.ds(0, planes * per)], mate_send.at[0]))
        for condition, head in heads:
            last = sum(cut[p + 1] - cut[p] for piece in pieces_of(head)[aslant_from(head):] for e, p in piece)
            pl.when(jnp.logical_and(slanted, condition))(
                functools.partial(gone, everyone.at[pl.ds(0, planes * per - last)], mate_send.at[0])
            )
            if last:
                pl.when(jnp.logical_and(slant, condition))(
                    functools.partial(gone, everyone.at[pl.ds(0, last)], slant_send.at[0])
                )
        pl.when(has_outer)(functools.partial(gone, everyone.at[pl.ds(0, planes * per)], outer_send.at[0]))
        gone(everyone.at[pl.ds(0, per)], cross_send.at[0])
        gone(everyone.at[pl.ds(0, per * (2 * cousins + 1))], col_send.at[0])
        for condition, copy in sent:
            if condition is None:
                copy.wait_send()
            else:
                pl.when(condition)(copy.wait_send)


def store_kernel(w_diag, w_near, w_cross, o_diag, o_near, o_cross, sem):
    copies = [
        pltpu.make_async_copy(w_diag, o_diag, sem.at[0]),
        pltpu.make_async_copy(w_near, o_near, sem.at[1]),
        pltpu.make_async_copy(w_cross, o_cross, sem.at[2]),
    ]
    for copy in copies:
        copy.start()
    for copy in copies:
        copy.wait()


def body(n, c, factor_t, intersection_diag, intersection_near, intersection_cross, near_cols, cross_cols):
    per, width, order = factor_t.shape
    near, cross = near_cols.shape[1], cross_cols.shape[1]
    planes = n // 4
    parts = max(1, min(PARTS // planes, per))
    col_parts = 1
    smem = pltpu.SMEM
    vmem = pl.BlockSpec(memory_space=pltpu.VMEM)
    hbm = pl.BlockSpec(memory_space=pl.ANY)
    dma = pltpu.SemaphoreType.DMA
    shapes = ((per, width, order), (per, near, width, order), (per, cross, width, order))
    kept = 2 * order * width * per * (1 + near + cross)
    results = pl.pallas_call(
        functools.partial(refine_kernel, n, c, parts),
        out_shape=tuple(pltpu.VMEM(shape, BF16) for shape in shapes),
        in_specs=[pl.BlockSpec(memory_space=pltpu.HBM)] * 6,
        out_specs=(vmem,) * 3,
        scratch_shapes=[
            pltpu.VMEM((n * per, width, order), BF16),
            pltpu.VMEM((3 * per, width, order), BF16),
            pltpu.VMEM((per, near + cross, order, order), BF16),
            pltpu.VMEM((per, order, order), BF16),
            pltpu.VMEM(intersection_diag.shape, BF16),
            pltpu.VMEM(intersection_near.shape, BF16),
            pltpu.VMEM(intersection_cross.shape, BF16),
            smem((near, per), jnp.int32),
            smem((cross, per), jnp.int32),
            dma((5,)),
            dma((2,)),
            dma((1,)),
            dma((c, col_parts)),
            dma((2,)),
            dma((2,)),
            dma((1,)),
            dma((1,)),
            dma((1,)),
            dma((1,)),
            dma((planes, parts)),
            dma((planes,)),
            pltpu.SemaphoreType.REGULAR((4 + c // 2,)),
        ],
        compiler_params=pltpu.CompilerParams(
            collective_id=0, has_side_effects=True, vmem_limit_bytes=VMEM_ALL - kept - SLACK,
        ),
    )(factor_t, intersection_diag, intersection_near, intersection_cross, near_cols.T, cross_cols.T)
    return pl.pallas_call(
        store_kernel,
        out_shape=tuple(jax.ShapeDtypeStruct(shape, BF16) for shape in shapes),
        in_specs=[vmem] * 3,
        out_specs=(hbm,) * 3,
        scratch_shapes=[dma((3,))],
        compiler_params=pltpu.CompilerParams(vmem_limit_bytes=VMEM_LIMIT),
    )(*results)


def solution(mesh):
    placed = (
        P("rows", "col", None),
        P("rows", None, None),
        P("rows", None, None, None),
        P("rows", None, None, None),
        P("rows", None),
        P("rows", None),
    )
    return jax.shard_map(
        functools.partial(body, mesh.shape["rows"], mesh.shape["col"]),
        mesh=mesh,
        in_specs=placed,
        out_specs=(
            P("rows", "col", None),
            P("rows", None, "col", None),
            P("rows", None, "col", None),
        ),
        check_vma=False,
    )
```

```python
import functools

import jax
import jax.numpy as jnp
from jax import lax
from jax.experimental import pallas as pl
from jax.experimental.pallas import tpu as pltpu
from jax.sharding import PartitionSpec as P

F32 = jnp.float32
BF16 = jnp.bfloat16
PARTS = 14
ROW_CUT = (0, 5, 10, 14)
VMEM_LIMIT = 16 * 1024 * 1024
VMEM_ALL = 67043328
SLACK = 96 * 1024
NT = (((1,), (1,)), ((), ()))
TN = (((0,), (0,)), ((), ()))


def dot(a, b, dims=(((1,), (0,)), ((), ()))):
    return lax.dot_general(a, b, dims, preferred_element_type=F32)


def split(rows, parts):
    size = rows // parts
    return [pl.ds(p * size, size) for p in range(parts)]


def refine_kernel(
    n, c, parts,
    factor, s_diag, s_near, s_cross, near_cols, cross_cols,
    w_diag, w_near, w_cross,
    everyone, nearby, g, full, v_diag, v_near, v_cross, near_at, cross_at,
    load_sem, own_sem, col_send, col_recv, near_send, near_recv,
    cross_send, outer_send, mate_send, slant_send, chain_recv, mate_recv, ready,
):
    per, width, order = factor.shape
    near, cross = v_near.shape[1], v_cross.shape[1]
    half = n // 2
    planes = half // 2
    cut = [per * p // parts for p in range(parts + 1)]
    r = lax.axis_index("rows")
    q = lax.axis_index("col")
    upper = r // half
    is_upper = upper == 1
    m = r - upper * half
    s = m % 2
    d = jnp.where(is_upper, m // 2, planes - 1 - m // 2)
    inmost = d == 0
    beyond = d > 0
    lower_inmost = jnp.logical_and(upper == 0, inmost)
    upper_inmost = jnp.logical_and(is_upper, inmost)
    has_outer = d + 1 < planes
    first_core = q % 2 == 0
    mate = r + 1 - 2 * s
    target = jnp.where(is_upper, half - 2 + s, half + s)
    outer = jnp.where(is_upper, r + 2, r - 2)
    col_mate = q + 1 - 2 * (q % 2)
    col_cousins = [(q + 2 * k) % c for k in range(1, c // 2)]
    cousins = len(col_cousins)
    origin = jnp.logical_and(r == 0, q == 0)
    CORE, MATE, NEXT, CROSS, SLANT, COUSIN = 0, 1, 2, 3, 4, 5

    def other_row(e, side):
        return jnp.where(is_upper, half - 2 - 2 * e, half + 2 * e) + side

    loads = [
        pltpu.make_async_copy(s_diag, v_diag, load_sem.at[0]),
        pltpu.make_async_copy(s_near, v_near, load_sem.at[1]),
        pltpu.make_async_copy(s_cross, v_cross, load_sem.at[2]),
        pltpu.make_async_copy(near_cols, near_at, load_sem.at[3]),
        pltpu.make_async_copy(cross_cols, cross_at, load_sem.at[4]),
    ]

    def beside(step):
        return nearby.at[pl.ds((1 + step) * per, per)]

    own_near = pltpu.make_async_copy(factor, beside(0), own_sem.at[0])

    def rows_of(column):
        return pl.ds(pl.multiple_of(column * width, width), width)

    own_full = pltpu.make_async_copy(factor, full.at[:, rows_of(q), :], own_sem.at[1])

    barrier = pltpu.get_barrier_semaphore()

    def signal(sem, **where):
        pl.semaphore_signal(sem, inc=1, device_id=where, device_id_type=pl.DeviceIdType.MESH)

    greets = [
        (jnp.logical_or(q < col_mate, jnp.logical_and(r == 0, col_mate == 0)), {"col": col_mate}),
        (s == 0, {"rows": mate}),
        (jnp.logical_and(upper == 0, m + 2 < half), {"rows": r + 2}),
        (jnp.logical_and(upper == 0, beyond), {"rows": half + s}),
    ] + [(lower_inmost, {"rows": half + 2 * e + s}) for e in range(planes)]
    greets += [(q < column, {"col": column}) for column in col_cousins]
    late_greets = [(jnp.logical_and(is_upper, m + 2 < half), {"rows": r + 2})]
    heard = [jnp.logical_or(q > col_mate, origin), s == 1, m >= 2, is_upper] + [q > column for column in col_cousins]
    heard += [upper_inmost] * (planes - 1)
    answers = [
        (q > col_mate, CORE, {"col": col_mate}),
        (s == 1, MATE, {"rows": mate}),
        (m >= 2, NEXT, {"rows": r - 2}),
    ] + [(upper_inmost, CROSS, {"rows": half - 2 - 2 * e + s}) for e in range(planes)]
    answers += [(q > column, COUSIN + cousins - 1 - k, {"col": column}) for k, column in enumerate(col_cousins)]

    for condition, where in greets:
        pl.when(condition)(functools.partial(signal, barrier, **where))

    own_full.start()
    own_near.start()
    for load in loads:
        load.start()
    with jax.named_scope("bar"):
        pl.semaphore_wait(barrier, sum(x.astype(jnp.int32) for x in heard))
    for condition, where in late_greets:
        pl.when(condition)(functools.partial(signal, barrier, **where))
    for condition, k, where in answers:
        pl.when(condition)(functools.partial(signal, ready.at[k], **where))

    def send(src, dst, send_sem, recv_sem, **where):
        return pltpu.make_async_remote_copy(
            src_ref=src, dst_ref=dst, send_sem=send_sem, recv_sem=recv_sem,
            device_id=where, device_id_type=pl.DeviceIdType.MESH,
        )

    halves = split(per, col_recv.shape[1])

    def column_piece(column, h):
        return full.at[halves[h], rows_of(column), :]

    def slot(row, p):
        return everyone.at[pl.ds(row * per + cut[p], cut[p + 1] - cut[p])]

    crossing = [
        send(
            factor.at[pl.ds(cut[p], cut[p + 1] - cut[p])], slot(r, p),
            cross_send.at[0], chain_recv.at[d, p], rows=target,
        )
        for p in range(parts)
    ]
    toward = 1 - 2 * s
    to_mate = [send(factor, beside(-toward), near_send.at[0], near_recv.at[0], rows=mate)]
    to_core = [
        send(factor.at[halves[h]], column_piece(q, h), col_send.at[0], col_recv.at[q, h], col=col_mate)
        for h in range(len(halves))
    ]
    to_cousins = [
        [
            send(factor.at[halves[h]], column_piece(q, h), col_send.at[0], col_recv.at[q, h], col=column)
            for h in range(len(halves))
        ]
        for k, column in enumerate(col_cousins)
    ]
    firsts = [(is_upper, None, crossing), (s == 1, MATE, to_mate)]
    firsts += [(q > column, COUSIN + k, to_cousins[k]) for k, column in enumerate(col_cousins)]
    firsts += [(q > col_mate, CORE, to_core)]

    def start_all(copies):
        for copy in copies:
            copy.start()

    with jax.named_scope("own"):
        for condition, _, copies in firsts:
            pl.when(condition)(functools.partial(start_all, copies))

        def after_answer(k, copies):
            pl.semaphore_wait(ready.at[k], 1)
            start_all(copies)

        for condition, k, copies in firsts[:0:-1]:
            pl.when(jnp.logical_not(condition))(functools.partial(after_answer, k, copies))
        pl.when(jnp.logical_and(jnp.logical_and(lower_inmost, has_outer), s == 0))(
            functools.partial(signal, ready.at[SLANT], rows=mate)
        )
        pl.when(upper == 0)(functools.partial(after_answer, CROSS, crossing))
        pl.when(m + 2 < half)(lambda: pl.semaphore_wait(ready.at[NEXT], 1))

    sent = [(None, copy) for copy in to_mate]

    def landed(ref, sem):
        send(ref, ref, near_send.at[0], sem, rows=mate).wait_recv()

    def spread(e, p):
        ref = slot(other_row(e, s), p)
        return (
            send(ref, ref, outer_send.at[0], chain_recv.at[e, p], rows=outer),
            send(ref, ref, mate_send.at[0], mate_recv.at[e], rows=mate),
        )

    def forward(e, p):
        landed(slot(other_row(e, s), p), chain_recv.at[e, p])
        on, across = spread(e, p)
        pl.when(has_outer)(on.start)
        across.start()

    slant = jnp.logical_and(jnp.logical_and(lower_inmost, has_outer), s == 1)
    slanted = jnp.logical_and(jnp.logical_and(upper == 0, d == 1), s == 1)

    def forward_last(e, p):
        ref = slot(other_row(e, s), p)
        landed(ref, chain_recv.at[e, p])
        on, across = spread(e, p)
        aslant = send(ref, ref, slant_send.at[0], mate_recv.at[e], rows=outer - 1)
        pl.when(slant)(aslant.start)
        pl.when(jnp.logical_and(has_outer, jnp.logical_not(slant)))(on.start)
        pl.when(jnp.logical_not(slanted))(across.start)

    def near_copy(src_ref, step, row):
        return send(src_ref, beside(step), near_send.at[1], near_recv.at[1], rows=row)

    passing = near_copy(beside(toward), -toward, r + 2 * toward)
    prompt = jnp.logical_and(lower_inmost, first_core)
    passes = jnp.logical_and(jnp.where(s == 1, m >= 2, m + 2 < half), jnp.logical_not(jnp.logical_and(prompt, s == 1)))
    direct = near_copy(factor, 1, r - 1)
    directs = jnp.logical_and(jnp.logical_and(prompt, s == 0), m >= 2)
    sent += [(passes, passing), (directs, direct)]

    def pass_near(where):
        pl.when(jnp.logical_and(where, passes))(passing.start)
        pl.when(jnp.logical_and(where, directs))(direct.start)

    def arrive_column(column, h):
        landed(column_piece(column, h), col_recv.at[column, h])

    eye = (
        lax.broadcasted_iota(jnp.int32, (width, order), 0) + q * width
        == lax.broadcasted_iota(jnp.int32, (width, order), 1)
    ).astype(F32)

    def prepare(i, carry):
        z_t = full[i]
        own = full[i, rows_of(q), :]
        square = (-0.5 * dot(z_t, z_t, TN)).astype(BF16)
        blocks = [v_near[i, k] for k in range(near)] + [v_cross[i, k] for k in range(cross)]
        tall = dot(jnp.concatenate(blocks, axis=1), square, TN).astype(BF16)
        for k in range(near + cross):
            g[i, k] = tall[k * order:(k + 1) * order]
        product = dot(own, v_diag[i], NT).astype(BF16)
        residual = (eye - dot(product, z_t, NT)).astype(BF16)
        w_diag[i] = (own.astype(F32) + 0.5 * dot(residual, z_t)).astype(BF16)
        return carry

    def rows_from(e):
        return everyone.at[pl.ds(other_row(e, 1 - s) * per, per)]

    chunks = [(e, p) for e in range(planes) for p in range(parts)]

    def forwards(first, last):
        for e, p in chunks[first:last]:
            with jax.named_scope(f"x{e}{p}"):
                forward(e, p)

    def pass_columns():
        for h in range(len(halves)):
            for k, column in enumerate(col_cousins):
                arrive_column(column, h)
                ref = column_piece(column, h)
                send(ref, ref, col_send.at[0], col_recv.at[column, h], col=col_mate).start()

    heads = [
        (jnp.logical_and(first_core, upper == 0), 1),
        (jnp.logical_and(first_core, is_upper), 0),
        (jnp.logical_not(first_core), max(1, parts * 3 // 4)),
    ]

    middle = len(chunks) - parts - (parts * 3 // 5)

    def pieces_of(head):
        passing = chunks[parts:]
        return chunks[:head], passing[:middle], passing[middle:], chunks[head:parts]

    def aslant_from(head):
        return 2 if head == 1 else 3

    def take(where, *places):
        for condition, head in heads:
            def some():
                last = []
                for place in places:
                    for e, p in pieces_of(head)[place]:
                        with jax.named_scope(f"x{e}{p}"):
                            if place < aslant_from(head):
                                forward(e, p)
                            else:
                                forward_last(e, p)
                                last.append(spread(e, p)[0])
                if last:
                    pl.when(slant)(functools.partial(start_all, last))
            pl.when(jnp.logical_and(where, condition))(some)

    beyond_first = jnp.logical_and(beyond, first_core)
    beyond_second = jnp.logical_and(beyond, jnp.logical_not(first_core))

    def spread_rows(step, first, last):
        with jax.named_scope(f"prep{step}"):
            lax.fori_loop(first, last, prepare, 0, unroll=True)

    take(inmost, 0)
    with jax.named_scope("colf"):
        pass_columns()
    take(inmost, 1)
    take(beyond_second, 0)
    pl.when(slant)(lambda: pl.semaphore_wait(ready.at[SLANT], 1))
    take(inmost, 2, 3)
    pass_near(prompt)
    with jax.named_scope("loads"):
        own_full.wait()
        for load in loads:
            load.wait()
    with jax.named_scope("cols"):
        for h in range(len(halves)):
            arrive_column(col_mate, h)
            for k in range(1, c // 2):
                arrive_column((col_mate + 2 * k) % c, h)

    row_cut = [per * k // 14 for k in ROW_CUT]
    spread_rows(0, row_cut[0], row_cut[1])
    take(beyond_first, 0)
    take(beyond_second, 1, 2)
    with jax.named_scope("near"):
        landed(beside(toward), near_recv.at[0])
        pass_near(jnp.logical_not(prompt))
    spread_rows(1, row_cut[1], row_cut[2])
    passes_on = jnp.logical_and(beyond, jnp.logical_not(slanted))
    take(beyond_first, 1)
    take(jnp.logical_and(passes_on, first_core), 2)
    take(passes_on, 3)
    spread_rows(2, row_cut[2], row_cut[3])

    with jax.named_scope("nwait"):
        own_near.wait()
        within = jnp.logical_and(m - toward >= 0, m - toward < half)
        edge = jnp.logical_and(jnp.logical_not(within), jnp.logical_and(r - toward >= 0, r - toward < n))
        pl.when(within)(functools.partial(landed, beside(-toward), near_recv.at[1]))

        @pl.when(edge)
        def _():
            landed(rows_from(0), mate_recv.at[0])
            copy = pltpu.make_async_copy(everyone.at[pl.ds((r - toward) * per, per)], beside(-toward), own_sem.at[0])
            copy.start()
            copy.wait()

    base = (r - 1) * per

    def finish_near(i, carry):
        for k in range(near):
            place = jnp.clip(near_at[k, i] - base, 0, 3 * per - 1)
            w_near[i, k] = dot(nearby[place], g[i, k]).astype(BF16)
        return carry

    def finish_cross(i, carry):
        for k in range(cross):
            w_cross[i, k] = dot(everyone[cross_at[k, i]], g[i, near + k]).astype(BF16)
        return carry

    with jax.named_scope("ndots"):
        lax.fori_loop(0, per, finish_near, 0, unroll=True)
    take(jnp.logical_and(slanted, first_core), 2)
    take(slanted, 3)
    with jax.named_scope("fin"):
        pl.when(jnp.logical_not(edge))(functools.partial(landed, rows_from(0), mate_recv.at[0]))
        for e in range(1, planes):
            landed(rows_from(e), mate_recv.at[e])
    with jax.named_scope("cdots"):
        lax.fori_loop(0, per, finish_cross, 0, unroll=True)
    with jax.named_scope("sends"):
        def gone(ref, sem):
            send(ref, ref, sem, near_recv.at[0], rows=mate).wait_send()

        pl.when(jnp.logical_not(slanted))(functools.partial(gone, everyone.at[pl.ds(0, planes * per)], mate_send.at[0]))
        for condition, head in heads:
            last = sum(cut[p + 1] - cut[p] for piece in pieces_of(head)[aslant_from(head):] for e, p in piece)
            pl.when(jnp.logical_and(slanted, condition))(
                functools.partial(gone, everyone.at[pl.ds(0, planes * per - last)], mate_send.at[0])
            )
            if last:
                pl.when(jnp.logical_and(slant, condition))(
                    functools.partial(gone, everyone.at[pl.ds(0, last)], slant_send.at[0])
                )
        pl.when(has_outer)(functools.partial(gone, everyone.at[pl.ds(0, planes * per)], outer_send.at[0]))
        gone(everyone.at[pl.ds(0, per)], cross_send.at[0])
        gone(everyone.at[pl.ds(0, per * (2 * cousins + 1))], col_send.at[0])
        for condition, copy in sent:
            if condition is None:
                copy.wait_send()
            else:
                pl.when(condition)(copy.wait_send)


def store_kernel(w_diag, w_near, w_cross, o_diag, o_near, o_cross, sem):
    copies = [
        pltpu.make_async_copy(w_diag, o_diag, sem.at[0]),
        pltpu.make_async_copy(w_near, o_near, sem.at[1]),
        pltpu.make_async_copy(w_cross, o_cross, sem.at[2]),
    ]
    for copy in copies:
        copy.start()
    for copy in copies:
        copy.wait()


def body(n, c, factor_t, intersection_diag, intersection_near, intersection_cross, near_cols, cross_cols):
    per, width, order = factor_t.shape
    near, cross = near_cols.shape[1], cross_cols.shape[1]
    planes = n // 4
    parts = max(1, min(PARTS // planes, per))
    col_parts = 1
    smem = pltpu.SMEM
    vmem = pl.BlockSpec(memory_space=pltpu.VMEM)
    hbm = pl.BlockSpec(memory_space=pl.ANY)
    dma = pltpu.SemaphoreType.DMA
    shapes = ((per, width, order), (per, near, width, order), (per, cross, width, order))
    kept = 2 * order * width * per * (1 + near + cross)
    results = pl.pallas_call(
        functools.partial(refine_kernel, n, c, parts),
        out_shape=tuple(pltpu.VMEM(shape, BF16) for shape in shapes),
        in_specs=[pl.BlockSpec(memory_space=pltpu.HBM)] * 6,
        out_specs=(vmem,) * 3,
        scratch_shapes=[
            pltpu.VMEM((n * per, width, order), BF16),
            pltpu.VMEM((3 * per, width, order), BF16),
            pltpu.VMEM((per, near + cross, order, order), BF16),
            pltpu.VMEM((per, order, order), BF16),
            pltpu.VMEM(intersection_diag.shape, BF16),
            pltpu.VMEM(intersection_near.shape, BF16),
            pltpu.VMEM(intersection_cross.shape, BF16),
            smem((near, per), jnp.int32),
            smem((cross, per), jnp.int32),
            dma((5,)),
            dma((2,)),
            dma((1,)),
            dma((c, col_parts)),
            dma((2,)),
            dma((2,)),
            dma((1,)),
            dma((1,)),
            dma((1,)),
            dma((1,)),
            dma((planes, parts)),
            dma((planes,)),
            pltpu.SemaphoreType.REGULAR((4 + c // 2,)),
        ],
        compiler_params=pltpu.CompilerParams(
            collective_id=0, has_side_effects=True, vmem_limit_bytes=VMEM_ALL - kept - SLACK,
        ),
    )(factor_t, intersection_diag, intersection_near, intersection_cross, near_cols.T, cross_cols.T)
    return pl.pallas_call(
        store_kernel,
        out_shape=tuple(jax.ShapeDtypeStruct(shape, BF16) for shape in shapes),
        in_specs=[vmem] * 3,
        out_specs=(hbm,) * 3,
        scratch_shapes=[dma((3,))],
        compiler_params=pltpu.CompilerParams(vmem_limit_bytes=VMEM_LIMIT),
    )(*results)


def solution(mesh):
    placed = (
        P("rows", "col", None),
        P("rows", None, None),
        P("rows", None, None, None),
        P("rows", None, None, None),
        P("rows", None),
        P("rows", None),
    )
    return jax.shard_map(
        functools.partial(body, mesh.shape["rows"], mesh.shape["col"]),
        mesh=mesh,
        in_specs=placed,
        out_specs=(
            P("rows", "col", None),
            P("rows", None, "col", None),
            P("rows", None, "col", None),
        ),
        check_vma=False,
    )
```
